32 devices in a mesh: echo: 2 (over y), gx: 4 (over z), gy: 2 (over x), gz: 2 (over core).
Axes of the slice: x: 2, y: 2, z: 4, core: 2. Of those that a mesh axis runs over, the one named last changes fastest.
Arguments:
- measured: bfloat16 [2, 32, 8, 16, 32], P(None, 'echo', 'gx', 'gy', 'gz'), parts along dimension 1, may hold values from -6 to 6
- sample_mask: int32 [16, 16, 32], P(('echo', 'gx'), 'gy', 'gz'), parts along dimension 0, may hold values 0 or 1
- kernel: bfloat16 [2, 5, 5, 5, 512], replicated, may hold values from -0.0625 to 0.0625
Outputs:
- spirit_kspace: bfloat16 [2, 32, 8, 16, 32], P(None, 'echo', 'gx', 'gy', 'gz'), parts along dimension 1
The draws below stay inside these ranges and needn't reach their ends.
There are 2 independent parts, one for each index of `echo`. The reference program is written for one: setup_inputs(seed, part) draws one part's arguments, and reference() takes and returns one part's arrays. A program takes and returns all parts, laid end to end along the dimension named above; an argument that names none is the same for every part. Nothing has to cross between parts.
All inputs are finite; a program needn't handle non-finite values. No bound on the sum of `sample_mask` on one device may be relied on, other than what follows from the above.
Results may differ from the reference program's by a relative error of at most 0.0016.
Values may be sent and summed in bfloat16 or wider, within the bound.
No kernel may reach another device: no remote copies, remote signals or barrier semaphores. Data moves between devices by JAX's collectives and lax.ppermute only.
A program may use at most 128 MiB of HBM per device.

```python
import jax
import jax.numpy as jnp
from jax import lax

COILS = 16
KS = 5
ITERS = 2
NX = 8
NY = 16
NZ = 32


def with_ends(array, key, smallest, largest):
    place = [jax.random.randint(jax.random.fold_in(key, axis), (), 0, length) for axis, length in enumerate(array.shape)]
    longest = array.shape.index(max(array.shape))
    next_to = place[:longest] + [(place[longest] + 1) % array.shape[longest]] + place[longest + 1:]
    return array.at[tuple(place)].set(smallest).at[tuple(next_to)].set(largest)


def block_levels(key, shape, split, low, high):
    loudness = 1.0
    for axis_at, shards_of in split:
        steps = jax.random.uniform(jax.random.fold_in(jax.random.fold_in(key, 6), axis_at), (shards_of,), jnp.float32, low / len(split), high / len(split))
        loudness = loudness * jnp.repeat(jnp.exp(steps), shape[axis_at] // shards_of).reshape((-1,) + (1,) * (len(shape) - 1 - axis_at))
    return loudness


def gaussian(key, dims, width, most, split=(), kind=jnp.bfloat16):
    values = jax.random.normal(key, dims, jnp.float32) * width
    if len(split) > 0:
        values = block_levels(key, dims, split, -0.22, 0.18) * values
    return jnp.clip(values, min=-most, max=most).astype(kind)


def setup_inputs(seed: int = 0, part: int = 0) -> dict:
    streams_of = jax.random.split(jax.random.key(seed), 4)
    part_keys = jax.random.split(jax.random.fold_in(streams_of[3], part), 4)
    measured = gaussian(part_keys[0], (2, COILS, NX, NY, NZ), 1.0, 6.0, ((2, 4), (3, 2), (4, 2)))
    sample_mask = with_ends((jax.random.randint(part_keys[1], (NX, NY, NZ), 0, 3) < 1).astype(jnp.int32), jax.random.fold_in(part_keys[1], 1), 0, 1)
    kernel = gaussian(streams_of[2], (2, KS, KS, KS, COILS * 2 * COILS), (4 * COILS * KS ** 3) ** -0.5, 0.0625)
    return {"measured": measured, "sample_mask": sample_mask, "kernel": kernel}


def unpack_kernel(kernel):
    shaped = kernel.reshape(2, KS, KS, KS, COILS, 2 * COILS)
    return jnp.transpose(shaped, (0, 4, 5, 1, 2, 3))


def tap_blocks(kernel):
    real_part = kernel[0].astype(jnp.float32)
    imag_part = kernel[1].astype(jnp.float32)
    upper_rows = jnp.concatenate([real_part, -imag_part], axis=1)
    lower_rows = jnp.concatenate([imag_part, real_part], axis=1)
    blocks = jnp.concatenate([upper_rows, lower_rows], axis=0)
    blocks = jnp.transpose(blocks, (2, 3, 4, 0, 1))
    return blocks.reshape(KS ** 3, blocks.shape[3], blocks.shape[4])


def conjugate_mirror(values):
    flipped = values[:, :, ::-1, ::-1, ::-1]
    return jnp.concatenate([flipped[:1], -flipped[1:]], axis=0)


def reference(measured, sample_mask, kernel):
    kernel = unpack_kernel(kernel)
    sampled = (sample_mask == 1)[None, None]
    current = jnp.where(sampled, measured, jnp.zeros_like(measured))
    blocks = tap_blocks(kernel)
    reach = KS // 2
    out_rows = 2 * COILS
    in_rows = 4 * COILS
    for iteration in range(ITERS):
        coils_all = jnp.concatenate([current, conjugate_mirror(current)], axis=1)
        coils_all = coils_all.astype(jnp.float32).reshape(in_rows, NX, NY, NZ)
        padded = jnp.pad(coils_all, ((0, 0), (reach, reach), (reach, reach), (reach, reach)))

        def add_tap(tap_index, running):
            tap_index = jnp.asarray(tap_index).astype(jnp.int32)
            offset_x = tap_index // (KS * KS)
            offset_y = (tap_index // KS) % KS
            offset_z = tap_index % KS
            start_zero = jnp.int32(0)
            window = lax.dynamic_slice(padded, (start_zero, offset_x, offset_y, offset_z), (in_rows, NX, NY, NZ))
            weights = lax.dynamic_slice(blocks, (tap_index, start_zero, start_zero), (1, out_rows, in_rows))[0]
            return running + jnp.einsum('oi,ixyz->oxyz', weights, window, precision=lax.Precision.HIGHEST)

        convolved = lax.fori_loop(0, KS ** 3, add_tap, jnp.zeros((out_rows, NX, NY, NZ), jnp.float32))
        convolved = convolved.reshape(2, COILS, NX, NY, NZ)
        current = jnp.where(sampled, measured.astype(jnp.float32), convolved).astype(jnp.bfloat16)
    return current
```

```python
import functools

import jax
import jax.numpy as jnp
from jax import lax
from jax.experimental import pallas as pl
from jax.experimental.pallas import tpu as pltpu
from jax.sharding import PartitionSpec as P

COILS = 16
KS = 5
ITERS = 2
SPACE = ("gx", "gy", "gz")
UNSAMPLED = 2.0 ** 100
LIMIT = 2.0 ** 99


def iota(shape, dim):
    return lax.broadcasted_iota(jnp.int32, shape, dim)


def one_hot(flags):
    return jnp.where(flags, 1.0, 0.0).astype(jnp.bfloat16)


def dot(a, b):
    return jnp.dot(a, b, preferred_element_type=jnp.float32)


def dot_nt(a, b):
    return lax.dot_general(a, b, (((1,), (1,)), ((), ())), preferred_element_type=jnp.float32)


def pack_kernel(measured_ref, mask_ref, packed_ref):
    parts, coils, size_x, size_y, size_z = measured_ref.shape
    lanes = size_y * size_z
    rows = parts * coils * size_y
    repeat = one_hot(iota((size_z, lanes), 1) % size_z == iota((size_z, lanes), 0))
    own_y = iota((rows, lanes), 1) // size_z == iota((rows, lanes), 0) % size_y
    gather = one_hot(iota((parts * coils, rows), 1) // size_y == iota((parts * coils, rows), 0))
    for x in range(size_x):
        values = measured_ref[:, :, x].astype(jnp.float32)
        sampled = (mask_ref[x] == 1)[None, None]
        coded = jnp.where(sampled, values, UNSAMPLED).reshape(rows, size_z).astype(jnp.bfloat16)
        spread = jnp.where(own_y, dot(coded, repeat), 0.0).astype(jnp.bfloat16)
        packed_ref[x * parts * coils : (x + 1) * parts * coils] = dot(gather, spread).astype(jnp.bfloat16)


def grid_kernel(sizes, blocks_ref, own_ref, taps_ref, place_ref, out_ref, flat, table, padded, coded):
    count_x, count_y, count_z = sizes
    parts, coils, local_x, local_y, local_z = out_ref.shape
    size_x, size_y, size_z = count_x * local_x, count_y * local_y, count_z * local_z
    channels = parts * coils
    width = size_x * channels
    reach = KS // 2
    taps = KS ** 3
    group = 128 // channels

    pair = 2 * coils
    per_tile = 128 // pair
    lane = iota((128, 256), 1)
    source = (lane // 128) * coils + lane % coils
    for c in range(coils):
        pick = one_hot(iota((128, 256), 0) == (c % per_tile) * pair + source)
        tile = (c // per_tile) * 128
        spread = dot(taps_ref[:, tile : tile + 128], pick)
        for half in range(2):
            rows_of_coil = pl.ds(c, taps_ref.shape[0], stride=coils)
            flat[half, rows_of_coil, :] = spread[:, half * 128 : half * 128 + 128]

    imaginary = iota((coils, 128), 1) // coils % 2 == 1
    lane_group = iota((channels, 128), 1) // channels

    def add_taps(step, carry):
        dy, dz = step // KS, step % KS
        for half in range(2):
            mats = []
            for dx in range(KS):
                tap = (dx * KS + dy) * KS + dz
                real_at = pl.multiple_of(tap * coils, coils)
                imag_at = pl.multiple_of((taps + tap) * coils, coils)
                real = flat[half, pl.ds(real_at, coils), :]
                imag = flat[half, pl.ds(imag_at, coils), :]
                if half == 0:
                    top = jnp.where(imaginary, -imag, real)
                    low = jnp.where(imaginary, real, imag)
                else:
                    top = jnp.where(imaginary, imag, real)
                    low = jnp.where(imaginary, -real, imag)
                mats.append(jnp.concatenate([top, low], axis=0).astype(jnp.bfloat16))
            known = {}
            zero = jnp.zeros((channels, 128), jnp.bfloat16)
            for x_out in range(size_x):
                for j in range(width // 128):
                    at = [j * group + g for g in range(group)]
                    if half == 1:
                        at = [size_x - 1 - a for a in at]
                    which = tuple(a - x_out + reach if 0 <= a - x_out + reach < KS else -1 for a in at)
                    if which not in known:
                        block = zero
                        for g, dx in enumerate(which):
                            if dx >= 0:
                                block = jnp.where(lane_group == g, mats[dx], block)
                        known[which] = block
                    start = pl.multiple_of(dz * 2 * width + half * width + j * 128, 128)
                    table[dy, x_out * channels : (x_out + 1) * channels, pl.ds(start, 128)] = known[which]
        return carry

    lax.fori_loop(0, KS * KS, add_taps, 0)

    half_rows = local_y * size_z
    row, col = iota((half_rows, half_rows), 0), iota((half_rows, half_rows), 1)
    block_size = local_y * local_z
    row_at = row // size_z * local_z + row % local_z + row % size_z // local_z * block_size
    order = one_hot(row_at == col)
    padded[: reach * size_z] = jnp.zeros((reach * size_z, padded.shape[1]), jnp.bfloat16)
    padded[(reach + size_y) * size_z :] = jnp.zeros((reach * size_z, padded.shape[1]), jnp.bfloat16)
    for gy in range(count_y):
        field = jnp.concatenate(
            [
                jnp.concatenate([blocks_ref[(gx * count_y + gy) * count_z + gz] for gz in range(count_z)], axis=1)
                for gx in range(count_x)
            ],
            axis=0,
        )
        coded[gy * half_rows : (gy + 1) * half_rows] = dot_nt(order, field)

    def spread(current):
        for dz in range(KS):
            shift = dz - reach
            inside = (row % size_z + shift >= 0) & (row % size_z + shift < size_z)
            direct = one_hot(inside & (col == row + shift))
            mirror = one_hot(inside & (half_rows - 1 - col == row + shift))
            for gy in range(count_y):
                values = current[gy]
                there = count_y - 1 - gy
                low = dz * 2 * width
                at = reach * size_z + gy * half_rows
                padded[at : at + half_rows, low : low + width] = dot(direct, values).astype(jnp.bfloat16)
                at = reach * size_z + there * half_rows
                padded[at : at + half_rows, low + width : low + 2 * width] = dot(mirror, values).astype(jnp.bfloat16)

    def known_values(gy):
        return coded[gy * half_rows : (gy + 1) * half_rows]

    current = []
    for gy in range(count_y):
        values = known_values(gy)
        current.append(jnp.where(values < LIMIT, values, 0.0).astype(jnp.bfloat16))
    for iteration in range(ITERS - 1):
        spread(current)
        total = jnp.zeros((size_y * size_z, width), jnp.float32)
        for dy in range(KS):
            total = total + dot_nt(padded[dy * size_z : (dy + size_y) * size_z], table[dy])
        current = []
        for gy in range(count_y):
            values = known_values(gy)
            part = total[gy * half_rows : (gy + 1) * half_rows]
            current.append(jnp.where(values < LIMIT, values, part).astype(jnp.bfloat16))
    spread(current)
    at_x, at_y, at_z = place_ref[0], place_ref[1], place_ref[2]
    own_rows = local_x * channels
    total = jnp.zeros((own_rows, local_y * local_z), jnp.float32)
    for dy in range(KS):
        pieces = []
        for y in range(local_y):
            start = pl.multiple_of((at_y * local_y + y + dy) * size_z + at_z * local_z, local_z)
            pieces.append(padded[pl.ds(start, local_z), :])
        window = jnp.concatenate(pieces, axis=0)
        weights = table[dy, pl.ds(pl.multiple_of(at_x * own_rows, own_rows), own_rows), :]
        total = total + dot_nt(weights, window)
    own = own_ref[...].astype(jnp.float32)
    result = jnp.where(own < LIMIT, own, total).astype(jnp.bfloat16)
    rows, lanes = channels * local_y, local_y * local_z
    unfold = one_hot(iota((rows, channels), 0) // local_y == iota((rows, channels), 1))
    own_y = iota((rows, lanes), 1) // local_z == iota((rows, lanes), 0) % local_y
    fold = one_hot(iota((lanes, local_z), 0) % local_z == iota((lanes, local_z), 1))
    for x in range(local_x):
        spread_out = dot(unfold, result[x * channels : (x + 1) * channels])
        spread_out = jnp.where(own_y, spread_out, 0.0).astype(jnp.bfloat16)
        values = dot(spread_out, fold).reshape(parts, coils, local_y, local_z)
        out_ref[:, :, x] = values.astype(jnp.bfloat16)


def gathered_body(measured, sample_mask, kernel):
    parts, coils, local_x, local_y, local_z = measured.shape
    sizes = tuple(lax.axis_size(axis) for axis in SPACE)
    devices = sizes[0] * sizes[1] * sizes[2]
    channels = parts * coils
    packed = pl.pallas_call(
        pack_kernel,
        out_shape=jax.ShapeDtypeStruct((local_x * channels, local_y * local_z), jnp.bfloat16),
        name="pack",
    )(measured, sample_mask)
    blocks = lax.all_to_all(jnp.broadcast_to(packed[None], (devices,) + packed.shape), SPACE, 0, 0)
    taps = kernel.reshape(parts * KS ** 3, coils * 2 * coils)
    taps = jnp.pad(taps, ((0, -taps.shape[0] % 16), (0, 0)))
    place = jnp.stack([lax.axis_index(axis) for axis in SPACE]).astype(jnp.int32)
    size_x, size_y, size_z = sizes[0] * local_x, sizes[1] * local_y, sizes[2] * local_z
    width = size_x * channels
    return pl.pallas_call(
        functools.partial(grid_kernel, sizes),
        out_shape=jax.ShapeDtypeStruct(measured.shape, jnp.bfloat16),
        in_specs=[pl.BlockSpec(memory_space=pltpu.VMEM)] * 3 + [pl.BlockSpec(memory_space=pltpu.SMEM)],
        out_specs=pl.BlockSpec(memory_space=pltpu.VMEM),
        scratch_shapes=[
            pltpu.VMEM((2, taps.shape[0] * coils, 128), jnp.float32),
            pltpu.VMEM((KS, width, 2 * KS * width), jnp.bfloat16),
            pltpu.VMEM(((size_y + 2 * (KS // 2)) * size_z, 2 * KS * width), jnp.bfloat16),
            pltpu.VMEM((size_y * size_z, width), jnp.float32),
        ],
        name="grid",
    )(blocks, packed, taps, place)


def partner(block, axis, bit):
    count = lax.axis_size(axis)
    route = []
    for low in range(count):
        high = low | 1 << bit
        if high != low and high < count:
            route += [(low, high), (high, low)]
    return lax.ppermute(block, axis, route)


def padded_2(shard, sides, width):
    for axis, dim in sides:
        size, length = (lax.axis_size(axis), shard.shape[dim])
        up = [(i, (i + 1) % size) for i in range(size - 1)]
        down = [(j, i) for i, j in up]
        last = lax.slice_in_dim(shard, length - width, length, axis=dim)
        leading = lax.slice_in_dim(shard, 0, width, axis=dim)
        before = lax.ppermute(last, axis, up)
        after = lax.ppermute(leading, axis, down)
        shard = jnp.concatenate([before, shard, after], axis=dim)
    return shard


def unpack_kernel(kernel):
    shaped = kernel.reshape(2, KS, KS, KS, COILS, 2 * COILS)
    return jnp.transpose(shaped, (0, 4, 5, 1, 2, 3))


def tap_matrix(kernel_part):
    real_part = kernel_part[0]
    imag_part = kernel_part[1]
    upper_rows = jnp.concatenate([real_part, -imag_part], axis=1)
    lower_rows = jnp.concatenate([imag_part, real_part], axis=1)
    blocks = jnp.concatenate([upper_rows, lower_rows], axis=0)
    return jnp.transpose(blocks, (2, 3, 0, 4, 1))


def conjugate(values):
    return jnp.concatenate([values[:1], -values[1:]], axis=0)


def convolve(padded, tap_table):
    extent = tap_table.shape[0]
    channel_count = padded.shape[0] * padded.shape[1]
    channels = padded.reshape((channel_count,) + padded.shape[2:])
    size_x = channels.shape[1] - extent + 1
    size_y = channels.shape[2] - extent + 1
    size_z = channels.shape[3] - extent + 1
    out_rows = tap_table.shape[2]
    running = jnp.zeros((out_rows, size_x * size_y * size_z), jnp.float32)
    for offset_x in range(extent):
        for offset_y in range(extent):
            pieces = [
                channels[
                    :,
                    offset_x : offset_x + size_x,
                    offset_y : offset_y + size_y,
                    offset_z : offset_z + size_z,
                ]
                for offset_z in range(extent)
            ]
            stacked = jnp.stack(pieces).reshape(extent * channel_count, size_x * size_y * size_z)
            weights = tap_table[offset_x, offset_y].reshape(out_rows, extent * channel_count)
            running = running + jnp.dot(weights, stacked, preferred_element_type=jnp.float32)
    return running.reshape(2, out_rows // 2, size_x, size_y, size_z)


def mirror_state(values):
    values = values[:, :, ::-1, ::-1, ::-1]
    for bit_place in range(lax.axis_size(("gx", "gy", "gz")).bit_length() - 1):
        values = partner(values, ("gx", "gy", "gz"), bit_place)
    return values


def halo_body(measured, sample_mask, kernel):
    kernel = unpack_kernel(kernel)
    reach = kernel.shape[-1] // 2
    sampled = (sample_mask == 1)[None, None]
    current = jnp.where(sampled, measured, jnp.zeros_like(measured))
    tap_table = tap_matrix(kernel)
    for iteration in range(ITERS):
        joined = jnp.concatenate([current, conjugate(mirror_state(current))], axis=1)
        padded = padded_2(joined, (("gx", 2), ("gy", 3), ("gz", 4)), reach)
        convolved = convolve(padded, tap_table)
        current = jnp.where(sampled, measured.astype(jnp.float32), convolved).astype(jnp.bfloat16)
    return current


def solution(mesh):
    grid = tuple(mesh.shape[axis] for axis in SPACE)
    spec = P(None, "echo", "gx", "gy", "gz")

    def body(measured, sample_mask, kernel):
        parts, coils, local_x, local_y, local_z = measured.shape
        width = grid[0] * local_x * parts * coils
        small = width == 256 and grid[1] == 2 and grid[1] * local_y * grid[2] * local_z <= 512
        if small:
            return gathered_body(measured, sample_mask, kernel)
        return halo_body(measured, sample_mask, kernel)

    return jax.shard_map(
        body,
        mesh=mesh,
        in_specs=(spec, P(("echo", "gx"), "gy", "gz"), P()),
        out_specs=spec,
        check_vma=False,
    )
```

```python
import functools

import jax
import jax.numpy as jnp
from jax import lax
from jax.experimental import pallas as pl
from jax.experimental.pallas import tpu as pltpu
from jax.sharding import PartitionSpec as P

COILS = 16
KS = 5
REACH = KS // 2
ITERS = 2
SPACE = ("gx", "gy", "gz")
UNSAMPLED = 2.0 ** 100
LIMIT = 2.0 ** 99
VMEM_LIMIT = 16 * 2 ** 20


def iota(shape, dim):
    return lax.broadcasted_iota(jnp.int32, shape, dim)


def one_hot(flags):
    return jnp.where(flags, 1.0, 0.0).astype(jnp.bfloat16)


def dot(a, b):
    return jnp.dot(a, b, preferred_element_type=jnp.float32)


def dot_nt(a, b):
    return lax.dot_general(a, b, (((1,), (1,)), ((), ())), preferred_element_type=jnp.float32)


def pack_kernel(measured_hbm, mask_hbm, packed_ref, measured_ref, mask_ref, sems):
    copies = [
        pltpu.make_async_copy(measured_hbm, measured_ref, sems.at[0]),
        pltpu.make_async_copy(mask_hbm, mask_ref, sems.at[1]),
    ]
    for copy in copies:
        copy.start()
    parts, coils, size_x, size_y, size_z = measured_ref.shape
    lanes = size_y * size_z
    rows = parts * coils * size_y
    repeat = one_hot(iota((size_z, lanes), 1) % size_z == iota((size_z, lanes), 0))
    own_y = iota((rows, lanes), 1) // size_z == iota((rows, lanes), 0) % size_y
    gather = one_hot(iota((parts * coils, rows), 1) // size_y == iota((parts * coils, rows), 0))
    for copy in copies:
        copy.wait()
    for x in range(size_x):
        values = measured_ref[:, :, x].astype(jnp.float32)
        sampled = (mask_ref[x] == 1)[None, None]
        coded = jnp.where(sampled, values, UNSAMPLED).reshape(rows, size_z).astype(jnp.bfloat16)
        spread = jnp.where(own_y, dot(coded, repeat), 0.0).astype(jnp.bfloat16)
        packed_ref[x * parts * coils : (x + 1) * parts * coils] = dot(gather, spread).astype(jnp.bfloat16)


def flat_kernel(taps_ref, flat):
    coils = COILS
    pair = 2 * coils
    per_tile = 128 // pair
    lane = iota((128, 256), 1)
    source = (lane // 128) * coils + lane % coils
    for c in range(coils):
        pick = one_hot(iota((128, 256), 0) == (c % per_tile) * pair + source)
        tile = (c // per_tile) * 128
        spread = dot(taps_ref[:, tile : tile + 128], pick)
        for half in range(2):
            rows_of_coil = pl.ds(c, taps_ref.shape[0], stride=coils)
            flat[half, rows_of_coil, :] = spread[:, half * 128 : half * 128 + 128]


def table_kernel(first_dy, size_x, flat, table):
    coils = COILS
    channels = 2 * coils
    width = size_x * channels
    taps = KS ** 3
    group = 128 // channels
    imaginary = iota((coils, 128), 1) // coils % 2 == 1
    lane_group = iota((channels, 128), 1) // channels

    def add_taps(step, carry):
        dy, dz = step // KS, step % KS
        for half in range(2):
            mats = []
            for dx in range(KS):
                tap = (dx * KS + dy + first_dy) * KS + dz
                real_at = pl.multiple_of(tap * coils, coils)
                imag_at = pl.multiple_of((taps + tap) * coils, coils)
                real = flat[half, pl.ds(real_at, coils), :]
                imag = flat[half, pl.ds(imag_at, coils), :]
                if half == 0:
                    top = jnp.where(imaginary, -imag, real)
                    low = jnp.where(imaginary, real, imag)
                else:
                    top = jnp.where(imaginary, imag, real)
                    low = jnp.where(imaginary, -real, imag)
                mats.append(jnp.concatenate([top, low], axis=0).astype(jnp.bfloat16))
            known = {}
            zero = jnp.zeros((channels, 128), jnp.bfloat16)
            for x_out in range(size_x):
                for j in range(width // 128):
                    at = [j * group + g for g in range(group)]
                    if half == 1:
                        at = [size_x - 1 - a for a in at]
                    which = tuple(a - x_out + REACH if 0 <= a - x_out + REACH < KS else -1 for a in at)
                    if which not in known:
                        block = zero
                        for g, dx in enumerate(which):
                            if dx >= 0:
                                block = jnp.where(lane_group == g, mats[dx], block)
                        known[which] = block
                    lanes = slice(half * width + j * 128, half * width + j * 128 + 128)
                    table[dy, dz, x_out * channels : (x_out + 1) * channels, lanes] = known[which]
        return carry

    lax.fori_loop(0, table.shape[0] * KS, add_taps, 0)


def order_kernel(local_y, local_z, size_z, order):
    rows = local_y * size_z
    row, col = iota((rows, rows), 0), iota((rows, rows), 1)

    def block_order(at):
        return at // size_z * local_z + at % local_z + at % size_z // local_z * (local_y * local_z)

    order[:rows] = one_hot(block_order(row) == col)
    order[rows : 2 * rows] = one_hot(block_order(rows - 1 - row) == col)
    order[2 * rows :] = one_hot(rows - 1 - row == col)


def grid_kernel(sizes, blocks_ref, measured_ref, mask_ref, order_ref, place_ref, *refs):
    tables, (out_ref, padded, coded) = refs[:-3], refs[-3:]
    table = [(ref, dy) for ref in tables for dy in range(ref.shape[0])]
    count_x, count_y, count_z = sizes
    parts, coils, local_x, local_y, local_z = out_ref.shape
    size_x, size_y, size_z = count_x * local_x, count_y * local_y, count_z * local_z
    channels = parts * coils
    width = size_x * channels
    at_x, at_y, at_z = place_ref[0], place_ref[1], place_ref[2]
    half_rows = local_y * size_z
    top = REACH * size_z

    def rows_of(gy):
        return slice(top + gy * half_rows, top + (gy + 1) * half_rows)

    edge = jnp.zeros((top, 2 * width), jnp.bfloat16)
    padded[:top] = edge
    padded[top + size_y * size_z :] = edge
    for gy in range(count_y):
        field = jnp.concatenate(
            [
                jnp.concatenate(
                    [
                        blocks_ref[((at_z ^ gz) * count_y + (at_y ^ gy)) * count_x + (at_x ^ gx)]
                        for gz in range(count_z)
                    ],
                    axis=1,
                )
                for gx in range(count_x)
            ],
            axis=0,
        )
        both = dot_nt(order_ref[: 2 * half_rows], field)
        coded[gy * half_rows : (gy + 1) * half_rows] = both[:half_rows]
        both = jnp.where(both < LIMIT, both, 0.0).astype(jnp.bfloat16)
        padded[rows_of(gy), :width] = both[:half_rows]
        padded[rows_of(count_y - 1 - gy), width:] = both[half_rows:]

    z_at = iota((size_y * size_z, width), 0) % size_z
    for iteration in range(ITERS - 1):
        total = None
        for dz in range(KS):
            part = None
            for dy, (ref, at) in enumerate(table):
                term = dot_nt(padded[dy * size_z : (dy + size_y) * size_z], ref[at, dz])
                part = term if part is None else part + term
            shift = dz - REACH
            if shift != 0:
                part = pltpu.roll(part, -shift % part.shape[0], 0)
                part = jnp.where((z_at + shift >= 0) & (z_at + shift < size_z), part, 0.0)
            total = part if total is None else total + part
        for gy in range(count_y):
            values = coded[gy * half_rows : (gy + 1) * half_rows]
            part = total[gy * half_rows : (gy + 1) * half_rows]
            values = jnp.where(values < LIMIT, values, part).astype(jnp.bfloat16)
            padded[rows_of(gy), :width] = values
            padded[rows_of(count_y - 1 - gy), width:] = dot(order_ref[2 * half_rows :], values).astype(jnp.bfloat16)

    own_rows = local_x * channels
    start_x = pl.multiple_of(at_x * own_rows, own_rows)
    result = None
    for dy, (ref, at) in enumerate(table):
        weights = jnp.concatenate([ref[at, dz, pl.ds(start_x, own_rows), :] for dz in range(KS)], axis=0)
        start = pl.multiple_of((at_y * local_y + dy) * size_z, size_z)
        term = dot_nt(weights, padded[pl.ds(start, half_rows), :])
        result = term if result is None else result + term
    z_at = iota((own_rows, half_rows), 1) % size_z
    total = None
    for dz in range(KS):
        part = result[dz * own_rows : (dz + 1) * own_rows]
        shift = dz - REACH
        if shift != 0:
            part = pltpu.roll(part, -shift % half_rows, 1)
            part = jnp.where((z_at + shift >= 0) & (z_at + shift < size_z), part, 0.0)
        total = part if total is None else total + part
    total = total.astype(jnp.bfloat16)

    rows = channels * local_y
    unfold = one_hot(iota((rows, channels), 0) // local_y == iota((rows, channels), 1))
    own_y = iota((rows, half_rows), 1) // size_z == iota((rows, half_rows), 0) % local_y
    fold = one_hot(iota((half_rows, local_z), 0) % size_z == at_z * local_z + iota((half_rows, local_z), 1))
    for x in range(local_x):
        spread_out = dot(unfold, total[x * channels : (x + 1) * channels])
        spread_out = jnp.where(own_y, spread_out, 0.0).astype(jnp.bfloat16)
        values = dot(spread_out, fold).reshape(parts, coils, local_y, local_z)
        sampled = (mask_ref[x] == 1)[None, None]
        values = jnp.where(sampled, measured_ref[:, :, x].astype(jnp.float32), values)
        out_ref[:, :, x] = values.astype(jnp.bfloat16)


def swap(block, axis, bit):
    count = lax.axis_size(axis)
    return lax.ppermute(block, axis, [(i, i ^ bit) for i in range(count)])


def gathered_body(measured, sample_mask, kernel):
    parts, coils, local_x, local_y, local_z = measured.shape
    sizes = tuple(lax.axis_size(axis) for axis in SPACE)
    devices = sizes[0] * sizes[1] * sizes[2]
    channels = parts * coils
    size_x, size_y, size_z = sizes[0] * local_x, sizes[1] * local_y, sizes[2] * local_z
    width = size_x * channels
    half_rows = local_y * size_z
    in_vmem = pl.BlockSpec(memory_space=pltpu.VMEM)
    in_hbm = pl.BlockSpec(memory_space=pltpu.HBM)

    def call(kernel_fn, name, out_shape, in_specs, scratch=(), limit=VMEM_LIMIT, cost=2 ** 22):
        return pl.pallas_call(
            kernel_fn,
            out_shape=out_shape,
            in_specs=in_specs,
            out_specs=in_vmem,
            scratch_shapes=list(scratch),
            compiler_params=pltpu.CompilerParams(vmem_limit_bytes=limit),
            cost_estimate=pl.CostEstimate(flops=0, bytes_accessed=cost, transcendentals=0),
            name=name,
        )

    packed = call(
        pack_kernel,
        "pack",
        jax.ShapeDtypeStruct((local_x * channels, local_y * local_z), jnp.bfloat16),
        [in_hbm, in_hbm],
        [
            pltpu.VMEM(measured.shape, measured.dtype),
            pltpu.VMEM(sample_mask.shape, sample_mask.dtype),
            pltpu.SemaphoreType.DMA((2,)),
        ],
    )(*[pltpu.with_memory_space_constraint(a, pltpu.HBM) for a in (measured, sample_mask)])

    def after(arrived, *work):
        return lax.optimization_barrier((arrived,) + work)

    taps = kernel.reshape(parts * KS ** 3, coils * 2 * coils)
    taps = jnp.pad(taps, ((0, -taps.shape[0] % 16), (0, 0)))
    place = jnp.stack([lax.axis_index(axis) for axis in SPACE]).astype(jnp.int32)
    steps = [(axis, 1 << bit) for axis in SPACE for bit in range(lax.axis_size(axis).bit_length() - 1)]
    blocks = packed[None]
    tables, order = [], None
    for number, (axis, bit) in enumerate(steps):
        arrived = swap(blocks, axis, bit)
        if number == 0:
            arrived, taps, place = after(arrived, taps, place)
        elif number == 1:
            flat_shape = jax.ShapeDtypeStruct((2, taps.shape[0] * coils, 128), jnp.float32)
            arrived, flat = after(arrived, call(flat_kernel, "flat", flat_shape, [in_vmem])(taps))
        elif number == 2:
            table_shape = jax.ShapeDtypeStruct((KS, KS, width, 2 * width), jnp.bfloat16)
            table = call(functools.partial(table_kernel, 0, size_x), "table", table_shape, [in_vmem])(flat)
            order_shape = jax.ShapeDtypeStruct((3 * half_rows, half_rows), jnp.bfloat16)
            order = call(functools.partial(order_kernel, local_y, local_z, size_z), "order", order_shape, [])()
            arrived, table, order = after(arrived, table, order)
            tables.append(table)
        blocks = jnp.concatenate([blocks, arrived], axis=0)

    return call(
        functools.partial(grid_kernel, sizes),
        "grid",
        jax.ShapeDtypeStruct(measured.shape, jnp.bfloat16),
        [in_vmem] * 4 + [pl.BlockSpec(memory_space=pltpu.SMEM)] + [in_vmem] * len(tables),
        [
            pltpu.VMEM(((size_y + 2 * REACH) * size_z, 2 * width), jnp.bfloat16),
            pltpu.VMEM((size_y * size_z, width), jnp.float32),
        ],
    )(blocks, measured, sample_mask, order, place, *tables)


def partner(block, axis, bit):
    count = lax.axis_size(axis)
    route = []
    for low in range(count):
        high = low | 1 << bit
        if high != low and high < count:
            route += [(low, high), (high, low)]
    return lax.ppermute(block, axis, route)


def padded_2(shard, sides, width):
    for axis, dim in sides:
        size, length = (lax.axis_size(axis), shard.shape[dim])
        up = [(i, (i + 1) % size) for i in range(size - 1)]
        down = [(j, i) for i, j in up]
        last = lax.slice_in_dim(shard, length - width, length, axis=dim)
        leading = lax.slice_in_dim(shard, 0, width, axis=dim)
        before = lax.ppermute(last, axis, up)
        after = lax.ppermute(leading, axis, down)
        shard = jnp.concatenate([before, shard, after], axis=dim)
    return shard


def unpack_kernel(kernel):
    shaped = kernel.reshape(2, KS, KS, KS, COILS, 2 * COILS)
    return jnp.transpose(shaped, (0, 4, 5, 1, 2, 3))


def tap_matrix(kernel_part):
    real_part = kernel_part[0]
    imag_part = kernel_part[1]
    upper_rows = jnp.concatenate([real_part, -imag_part], axis=1)
    lower_rows = jnp.concatenate([imag_part, real_part], axis=1)
    blocks = jnp.concatenate([upper_rows, lower_rows], axis=0)
    return jnp.transpose(blocks, (2, 3, 0, 4, 1))


def conjugate(values):
    return jnp.concatenate([values[:1], -values[1:]], axis=0)


def convolve(padded, tap_table):
    extent = tap_table.shape[0]
    channel_count = padded.shape[0] * padded.shape[1]
    channels = padded.reshape((channel_count,) + padded.shape[2:])
    size_x = channels.shape[1] - extent + 1
    size_y = channels.shape[2] - extent + 1
    size_z = channels.shape[3] - extent + 1
    out_rows = tap_table.shape[2]
    running = jnp.zeros((out_rows, size_x * size_y * size_z), jnp.float32)
    for offset_x in range(extent):
        for offset_y in range(extent):
            pieces = [
                channels[
                    :,
                    offset_x : offset_x + size_x,
                    offset_y : offset_y + size_y,
                    offset_z : offset_z + size_z,
                ]
                for offset_z in range(extent)
            ]
            stacked = jnp.stack(pieces).reshape(extent * channel_count, size_x * size_y * size_z)
            weights = tap_table[offset_x, offset_y].reshape(out_rows, extent * channel_count)
            running = running + jnp.dot(weights, stacked, preferred_element_type=jnp.float32)
    return running.reshape(2, out_rows // 2, size_x, size_y, size_z)


def mirror_state(values):
    values = values[:, :, ::-1, ::-1, ::-1]
    for bit_place in range(lax.axis_size(("gx", "gy", "gz")).bit_length() - 1):
        values = partner(values, ("gx", "gy", "gz"), bit_place)
    return values


def halo_body(measured, sample_mask, kernel):
    kernel = unpack_kernel(kernel)
    reach = kernel.shape[-1] // 2
    sampled = (sample_mask == 1)[None, None]
    current = jnp.where(sampled, measured, jnp.zeros_like(measured))
    tap_table = tap_matrix(kernel)
    for iteration in range(ITERS):
        joined = jnp.concatenate([current, conjugate(mirror_state(current))], axis=1)
        padded = padded_2(joined, (("gx", 2), ("gy", 3), ("gz", 4)), reach)
        convolved = convolve(padded, tap_table)
        current = jnp.where(sampled, measured.astype(jnp.float32), convolved).astype(jnp.bfloat16)
    return current


def solution(mesh):
    grid = tuple(mesh.shape[axis] for axis in SPACE)
    spec = P(None, "echo", "gx", "gy", "gz")

    def body(measured, sample_mask, kernel):
        parts, coils, local_x, local_y, local_z = measured.shape
        width = grid[0] * local_x * parts * coils
        small = width == 256 and grid[1] == 2 and local_y * grid[2] * local_z == 256
        if small:
            return gathered_body(measured, sample_mask, kernel)
        return halo_body(measured, sample_mask, kernel)

    return jax.shard_map(
        body,
        mesh=mesh,
        in_specs=(spec, P(("echo", "gx"), "gy", "gz"), P()),
        out_specs=spec,
        check_vma=False,
    )
```

```python
import functools

import jax
import jax.numpy as jnp
from jax import lax
from jax.experimental import pallas as pl
from jax.experimental.pallas import tpu as pltpu
from jax.sharding import PartitionSpec as P

COILS = 16
KS = 5
REACH = KS // 2
ITERS = 2
SPACE = ("gx", "gy", "gz")
UNSAMPLED = 2.0 ** 100
LIMIT = 2.0 ** 99
VMEM_LIMIT = 16 * 2 ** 20


def iota(shape, dim):
    return lax.broadcasted_iota(jnp.int32, shape, dim)


def one_hot(flags):
    return jnp.where(flags, 1.0, 0.0).astype(jnp.bfloat16)


def dot(a, b):
    return jnp.dot(a, b, preferred_element_type=jnp.float32)


def dot_nt(a, b):
    return lax.dot_general(a, b, (((1,), (1,)), ((), ())), preferred_element_type=jnp.float32)


def pack_kernel(measured_hbm, mask_hbm, packed_ref, measured_ref, mask_ref, sems):
    copies = [
        pltpu.make_async_copy(measured_hbm, measured_ref, sems.at[0]),
        pltpu.make_async_copy(mask_hbm, mask_ref, sems.at[1]),
    ]
    for copy in copies:
        copy.start()
    parts, coils, size_x, size_y, size_z = measured_ref.shape
    lanes = size_y * size_z
    rows = parts * coils * size_y
    repeat = one_hot(iota((size_z, lanes), 1) % size_z == iota((size_z, lanes), 0))
    own_y = iota((rows, lanes), 1) // size_z == iota((rows, lanes), 0) % size_y
    gather = one_hot(iota((parts * coils, rows), 1) // size_y == iota((parts * coils, rows), 0))
    for copy in copies:
        copy.wait()
    for x in range(size_x):
        values = measured_ref[:, :, x].astype(jnp.float32)
        sampled = (mask_ref[x] == 1)[None, None]
        coded = jnp.where(sampled, values, UNSAMPLED).reshape(rows, size_z).astype(jnp.bfloat16)
        spread = jnp.where(own_y, dot(coded, repeat), 0.0).astype(jnp.bfloat16)
        packed_ref[x * parts * coils : (x + 1) * parts * coils] = dot(gather, spread).astype(jnp.bfloat16)


def flat_kernel(taps_ref, flat):
    coils = COILS
    pair = 2 * coils
    per_tile = 128 // pair
    lane = iota((128, 256), 1)
    source = (lane // 128) * coils + lane % coils
    for c in range(coils):
        pick = one_hot(iota((128, 256), 0) == (c % per_tile) * pair + source)
        tile = (c // per_tile) * 128
        spread = dot(taps_ref[:, tile : tile + 128], pick)
        for half in range(2):
            rows_of_coil = pl.ds(c, taps_ref.shape[0], stride=coils)
            flat[half, rows_of_coil, :] = spread[:, half * 128 : half * 128 + 128]


def write_orders(order):
    rows = order.shape[1]
    row, col = iota((rows, rows), 0), iota((rows, rows), 1)
    order[:rows] = one_hot(row == col)
    order[rows:] = one_hot(rows - 1 - row == col)


def table_kernel(size_x, flat, table, order):
    write_orders(order)
    coils = COILS
    channels = 2 * coils
    width = size_x * channels
    group = 128 // channels
    imaginary = iota((coils, 128), 1) // coils % 2 == 1
    lane_group = iota((channels, 128), 1) // channels

    def add_taps(step, carry):
        dy, dz = step // KS, step % KS
        for half in range(2):
            mats = []
            for dx in range(KS):
                tap = (dx * KS + dy) * KS + dz
                real_at = pl.multiple_of(2 * tap * coils, coils)
                imag_at = pl.multiple_of((2 * tap + 1) * coils, coils)
                real = flat[half, pl.ds(real_at, coils), :]
                imag = flat[half, pl.ds(imag_at, coils), :]
                if half == 0:
                    top = jnp.where(imaginary, -imag, real)
                    low = jnp.where(imaginary, real, imag)
                else:
                    top = jnp.where(imaginary, imag, real)
                    low = jnp.where(imaginary, -real, imag)
                mats.append(jnp.concatenate([top, low], axis=0).astype(jnp.bfloat16))
            known = {}
            zero = jnp.zeros((channels, 128), jnp.bfloat16)
            for x_out in range(size_x):
                for j in range(width // 128):
                    at = [j * group + g for g in range(group)]
                    if half == 1:
                        at = [size_x - 1 - a for a in at]
                    which = tuple(a - x_out + REACH if 0 <= a - x_out + REACH < KS else -1 for a in at)
                    if which not in known:
                        block = zero
                        for g, dx in enumerate(which):
                            if dx >= 0:
                                block = jnp.where(lane_group == g, mats[dx], block)
                        known[which] = block
                    lanes = slice(half * width + j * 128, half * width + j * 128 + 128)
                    table[dy, dz, x_out * channels : (x_out + 1) * channels, lanes] = known[which]
        return carry

    lax.fori_loop(0, table.shape[0] * KS, add_taps, 0)


def load_half(sizes, blocks_ref, order_ref, place_ref, local_z, coded, points, mirrored):
    count_x, count_y, _ = sizes
    rows = order_ref.shape[1]
    edge = REACH * local_z
    field = jnp.concatenate(
        [
            jnp.concatenate(
                [blocks_ref[(place_ref[1] ^ gy) * count_x + (place_ref[0] ^ gx)] for gy in range(count_y)], axis=1
            )
            for gx in range(count_x)
        ],
        axis=0,
    )
    both = dot_nt(order_ref[...], field)
    coded[...] = both[:rows]
    both = jnp.where(both < LIMIT, both, 0.0).astype(jnp.bfloat16)
    for ref, values in ((points, both[:rows]), (mirrored, both[rows:])):
        ref[:edge] = jnp.zeros((edge, ref.shape[1]), jnp.bfloat16)
        ref[edge + rows :] = jnp.zeros((edge, ref.shape[1]), jnp.bfloat16)
        ref[edge : edge + rows] = values


def y_taps(ref, rows, local_z, weights):
    total = None
    for dy in range(KS):
        term = dot_nt(ref[dy * local_z : dy * local_z + rows], weights(dy))
        total = term if total is None else total + term
    return total


def near_kernel(sizes, local_z, blocks_ref, order_ref, place_ref, table, partial, coded, points, mirrored):
    rows, width = coded.shape
    load_half(sizes, blocks_ref, order_ref, place_ref, local_z, coded, points, mirrored)
    for dz in range(KS):
        partial[0, dz] = y_taps(points, rows, local_z, lambda dy: table[dy, dz, :, :width])
        partial[1, dz] = y_taps(mirrored, rows, local_z, lambda dy: table[dy, dz, :, width:])


def shift_z(own, other, shift, local_z, dim, own_first):
    length = own.shape[dim]
    inside = iota(own.shape, dim) % local_z + shift
    inside = (inside >= 0) & (inside < local_z)
    across = pltpu.roll(other, (local_z - shift if shift > 0 else -local_z - shift) % length, dim)
    keep = own_first if shift > 0 else 1.0 - own_first
    return jnp.where(inside, pltpu.roll(own, -shift % length, dim), across * keep)


def grid_kernel(
    sizes, blocks_ref, measured_ref, mask_ref, order_ref, place_ref, table, partial, coded_near,
    out_ref, coded_far, points, mirrored, near, far, lined,
):
    parts, coils, local_x, local_y, local_z = out_ref.shape
    channels = parts * coils
    rows, width = coded_far.shape
    at_x, at_y = place_ref[0], place_ref[1]
    own_first = (1 - place_ref[2]).astype(jnp.float32)
    edge = REACH * local_z
    load_half(sizes, blocks_ref, order_ref, place_ref, local_z, coded_far, points, mirrored)
    for iteration in range(ITERS - 1):
        totals = [None, None]
        for dz in sorted(range(KS), key=lambda dz: dz == REACH):
            shift = dz - REACH
            own = partial[0, dz] + y_taps(mirrored, rows, local_z, lambda dy: table[dy, dz, :, width:])
            other = partial[1, dz] + y_taps(points, rows, local_z, lambda dy: table[dy, dz, :, :width])
            if shift != 0:
                own, other = (
                    shift_z(own, other, shift, local_z, 0, own_first),
                    shift_z(other, own, shift, local_z, 0, 1.0 - own_first),
                )
            totals = [part if total is None else total + part for total, part in zip(totals, (own, other))]
        for ref, mirror_ref, coded, total in ((near, far, coded_near, totals[0]), (far, near, coded_far, totals[1])):
            values = jnp.where(coded[...] < LIMIT, coded[...], total).astype(jnp.bfloat16)
            ref[edge : edge + rows, :width] = values
            mirror_ref[edge : edge + rows, width:] = dot(order_ref[rows:], values).astype(jnp.bfloat16)
    for ref in (near, far):
        ref[:edge] = jnp.zeros((edge, 2 * width), jnp.bfloat16)
        ref[edge + rows :] = jnp.zeros((edge, 2 * width), jnp.bfloat16)

    own_rows = local_x * channels
    own_points = local_y * local_z
    start_x = pl.multiple_of(at_x * own_rows, own_rows)
    result = None
    for dy in range(KS):
        weights = jnp.concatenate([table[dy, dz, pl.ds(start_x, own_rows), :] for dz in range(KS)], axis=0)
        start = pl.multiple_of((at_y * local_y + dy) * local_z, local_z)
        window = jnp.concatenate([near[pl.ds(start, own_points), :], far[pl.ds(start, own_points), :]], axis=0)
        term = dot_nt(weights, window)
        result = term if result is None else result + term
    total = None
    for dz in range(KS):
        own = result[dz * own_rows : (dz + 1) * own_rows, :own_points]
        other = result[dz * own_rows : (dz + 1) * own_rows, own_points:]
        if dz != REACH:
            own = shift_z(own, other, dz - REACH, local_z, 1, own_first)
        total = own if total is None else total + own

    for y in range(local_y):
        piece = total if y == 0 else pltpu.roll(total, own_points - y * local_z, 1)
        lined[pl.ds(y, own_rows, stride=local_y), :] = piece
    for x in range(local_x):
        values = lined[x * channels * local_y : (x + 1) * channels * local_y, :local_z]
        values = values.reshape(parts, coils, local_y, local_z)
        sampled = (mask_ref[x] == 1)[None, None]
        values = jnp.where(sampled, measured_ref[:, :, x].astype(jnp.float32), values)
        out_ref[:, :, x] = values.astype(jnp.bfloat16)


def swap(block, axis, bit):
    count = lax.axis_size(axis)
    return lax.ppermute(block, axis, [(i, i ^ bit) for i in range(count)])


def gathered_body(measured, sample_mask, kernel):
    parts, coils, local_x, local_y, local_z = measured.shape
    sizes = tuple(lax.axis_size(axis) for axis in SPACE)
    devices = sizes[0] * sizes[1] * sizes[2]
    channels = parts * coils
    size_x, size_y, size_z = sizes[0] * local_x, sizes[1] * local_y, sizes[2] * local_z
    width = size_x * channels
    half_rows = size_y * local_z
    in_vmem = pl.BlockSpec(memory_space=pltpu.VMEM)
    in_hbm = pl.BlockSpec(memory_space=pltpu.HBM)

    def call(kernel_fn, name, out_shape, in_specs, scratch=(), outs=1, cost=2 ** 22):
        return pl.pallas_call(
            kernel_fn,
            out_shape=out_shape,
            in_specs=in_specs,
            out_specs=in_vmem if outs == 1 else (in_vmem,) * outs,
            scratch_shapes=list(scratch),
            compiler_params=pltpu.CompilerParams(vmem_limit_bytes=VMEM_LIMIT),
            cost_estimate=pl.CostEstimate(flops=0, bytes_accessed=cost, transcendentals=0),
            name=name,
        )

    packed = call(
        pack_kernel,
        "pack",
        jax.ShapeDtypeStruct((local_x * channels, local_y * local_z), jnp.bfloat16),
        [in_hbm, in_hbm],
        [
            pltpu.VMEM(measured.shape, measured.dtype),
            pltpu.VMEM(sample_mask.shape, sample_mask.dtype),
            pltpu.SemaphoreType.DMA((2,)),
        ],
    )(*[pltpu.with_memory_space_constraint(a, pltpu.HBM) for a in (measured, sample_mask)])

    def after(arrived, *work):
        return lax.optimization_barrier((arrived,) + work)

    taps = jnp.moveaxis(kernel, 0, 3).reshape(parts * KS ** 3, coils * 2 * coils)
    taps = jnp.pad(taps, ((0, -taps.shape[0] % 16), (0, 0)))
    place = jnp.stack([lax.axis_index(axis) for axis in SPACE]).astype(jnp.int32)
    steps = [(axis, 1 << bit) for axis in SPACE for bit in range(lax.axis_size(axis).bit_length() - 1)]
    blocks = packed[None]
    table, order = None, None
    for number, (axis, bit) in enumerate(steps):
        arrived = swap(blocks, axis, bit)
        if number == 0:
            arrived, taps, place = after(arrived, taps, place)
        elif number == 1:
            flat_shape = jax.ShapeDtypeStruct((2, taps.shape[0] * coils, 128), jnp.float32)
            arrived, flat = after(arrived, call(flat_kernel, "flat", flat_shape, [in_vmem])(taps))
        elif number == 2:
            table_shape = jax.ShapeDtypeStruct((KS, KS, width, 2 * width), jnp.bfloat16)
            order_shape = jax.ShapeDtypeStruct((2 * half_rows, half_rows), jnp.bfloat16)
            table_fn = functools.partial(table_kernel, size_x)
            table, order = call(table_fn, "table", (table_shape, order_shape), [in_vmem], outs=2)(flat)
            arrived, table, order = after(arrived, table, order)
        elif number == len(steps) - 1:
            in_smem = pl.BlockSpec(memory_space=pltpu.SMEM)
            padded_rows = half_rows + 2 * REACH * local_z
            padded = pltpu.VMEM((padded_rows, width), jnp.bfloat16)
            partial_shape = jax.ShapeDtypeStruct((2, KS, half_rows, width), jnp.float32)
            coded_shape = jax.ShapeDtypeStruct((half_rows, width), jnp.float32)
            partial, coded = call(
                functools.partial(near_kernel, sizes, local_z),
                "near",
                (partial_shape, coded_shape),
                [in_vmem, in_vmem, in_smem, in_vmem],
                [padded, padded],
                outs=2,
            )(blocks, order, place, table)
            arrived, partial, coded = after(arrived, partial, coded)
            break
        blocks = jnp.concatenate([blocks, arrived], axis=0)

    both = pltpu.VMEM((padded_rows, 2 * width), jnp.bfloat16)
    return call(
        functools.partial(grid_kernel, sizes),
        "grid",
        jax.ShapeDtypeStruct(measured.shape, jnp.bfloat16),
        [in_vmem] * 4 + [in_smem] + [in_vmem] * 3,
        [
            pltpu.VMEM((half_rows, width), jnp.float32),
            padded,
            padded,
            both,
            both,
            pltpu.VMEM((local_x * channels * local_y, 128), jnp.float32),
        ],
    )(arrived, measured, sample_mask, order, place, table, partial, coded)


def partner(block, axis, bit):
    count = lax.axis_size(axis)
    route = []
    for low in range(count):
        high = low | 1 << bit
        if high != low and high < count:
            route += [(low, high), (high, low)]
    return lax.ppermute(block, axis, route)


def padded_2(shard, sides, width):
    for axis, dim in sides:
        size, length = (lax.axis_size(axis), shard.shape[dim])
        up = [(i, (i + 1) % size) for i in range(size - 1)]
        down = [(j, i) for i, j in up]
        last = lax.slice_in_dim(shard, length - width, length, axis=dim)
        leading = lax.slice_in_dim(shard, 0, width, axis=dim)
        before = lax.ppermute(last, axis, up)
        after = lax.ppermute(leading, axis, down)
        shard = jnp.concatenate([before, shard, after], axis=dim)
    return shard


def unpack_kernel(kernel):
    shaped = kernel.reshape(2, KS, KS, KS, COILS, 2 * COILS)
    return jnp.transpose(shaped, (0, 4, 5, 1, 2, 3))


def tap_matrix(kernel_part):
    real_part = kernel_part[0]
    imag_part = kernel_part[1]
    upper_rows = jnp.concatenate([real_part, -imag_part], axis=1)
    lower_rows = jnp.concatenate([imag_part, real_part], axis=1)
    blocks = jnp.concatenate([upper_rows, lower_rows], axis=0)
    return jnp.transpose(blocks, (2, 3, 0, 4, 1))


def conjugate(values):
    return jnp.concatenate([values[:1], -values[1:]], axis=0)


def convolve(padded, tap_table):
    extent = tap_table.shape[0]
    channel_count = padded.shape[0] * padded.shape[1]
    channels = padded.reshape((channel_count,) + padded.shape[2:])
    size_x = channels.shape[1] - extent + 1
    size_y = channels.shape[2] - extent + 1
    size_z = channels.shape[3] - extent + 1
    out_rows = tap_table.shape[2]
    running = jnp.zeros((out_rows, size_x * size_y * size_z), jnp.float32)
    for offset_x in range(extent):
        for offset_y in range(extent):
            pieces = [
                channels[
                    :,
                    offset_x : offset_x + size_x,
                    offset_y : offset_y + size_y,
                    offset_z : offset_z + size_z,
                ]
                for offset_z in range(extent)
            ]
            stacked = jnp.stack(pieces).reshape(extent * channel_count, size_x * size_y * size_z)
            weights = tap_table[offset_x, offset_y].reshape(out_rows, extent * channel_count)
            running = running + jnp.dot(weights, stacked, preferred_element_type=jnp.float32)
    return running.reshape(2, out_rows // 2, size_x, size_y, size_z)


def mirror_state(values):
    values = values[:, :, ::-1, ::-1, ::-1]
    for bit_place in range(lax.axis_size(("gx", "gy", "gz")).bit_length() - 1):
        values = partner(values, ("gx", "gy", "gz"), bit_place)
    return values


def halo_body(measured, sample_mask, kernel):
    kernel = unpack_kernel(kernel)
    reach = kernel.shape[-1] // 2
    sampled = (sample_mask == 1)[None, None]
    current = jnp.where(sampled, measured, jnp.zeros_like(measured))
    tap_table = tap_matrix(kernel)
    for iteration in range(ITERS):
        joined = jnp.concatenate([current, conjugate(mirror_state(current))], axis=1)
        padded = padded_2(joined, (("gx", 2), ("gy", 3), ("gz", 4)), reach)
        convolved = convolve(padded, tap_table)
        current = jnp.where(sampled, measured.astype(jnp.float32), convolved).astype(jnp.bfloat16)
    return current


def solution(mesh):
    grid = tuple(mesh.shape[axis] for axis in SPACE)
    spec = P(None, "echo", "gx", "gy", "gz")

    def body(measured, sample_mask, kernel):
        parts, coils, local_x, local_y, local_z = measured.shape
        width = grid[0] * local_x * parts * coils
        points = grid[1] * local_y * local_z
        small = width == 256 and grid[1:] == (2, 2) and points == 256 and local_y * local_z == 128
        if small:
            return gathered_body(measured, sample_mask, kernel)
        return halo_body(measured, sample_mask, kernel)

    return jax.shard_map(
        body,
        mesh=mesh,
        in_specs=(spec, P(("echo", "gx"), "gy", "gz"), P()),
        out_specs=spec,
        check_vma=False,
    )
```

```python
import functools

import jax
import jax.numpy as jnp
from jax import lax
from jax.experimental import pallas as pl
from jax.experimental.pallas import tpu as pltpu
from jax.sharding import PartitionSpec as P

COILS = 16
KS = 5
REACH = KS // 2
ITERS = 2
SPACE = ("gx", "gy", "gz")
UNSAMPLED = 2.0 ** 100
LIMIT = 2.0 ** 99
VMEM_LIMIT = 16 * 2 ** 20


def iota(shape, dim):
    return lax.broadcasted_iota(jnp.int32, shape, dim)


def one_hot(flags):
    return jnp.where(flags, 1.0, 0.0).astype(jnp.bfloat16)


def dot(a, b):
    return jnp.dot(a, b, preferred_element_type=jnp.float32)


def dot_nt(a, b):
    return lax.dot_general(a, b, (((1,), (1,)), ((), ())), preferred_element_type=jnp.float32)


def pack_kernel(measured_hbm, mask_hbm, packed_ref, measured_ref, mask_ref, lined, sems):
    copies = [
        pltpu.make_async_copy(measured_hbm, measured_ref, sems.at[0]),
        pltpu.make_async_copy(mask_hbm, mask_ref, sems.at[1]),
    ]
    for copy in copies:
        copy.start()
    for copy in copies:
        copy.wait()
    parts, coils, size_x, size_y, size_z = measured_ref.shape
    channels = parts * coils
    rows = channels * size_y
    for x in range(size_x):
        values = measured_ref[:, :, x].astype(jnp.float32)
        sampled = (mask_ref[x] == 1)[None, None]
        lined[x, :, :size_z] = jnp.where(sampled, values, UNSAMPLED).reshape(rows, size_z)
    lane_y = iota((channels, size_y * size_z), 1) // size_z
    for x in range(size_x):
        packed = None
        for y in range(size_y):
            piece = lined[x, pl.ds(y, channels, stride=size_y), :]
            if y > 0:
                piece = jnp.where(lane_y == y, pltpu.roll(piece, y * size_z, 1), packed)
            packed = piece
        packed_ref[x * channels : (x + 1) * channels] = packed.astype(jnp.bfloat16)


def flat_kernel(taps_ref, flat):
    coils = COILS
    pair = 2 * coils
    per_tile = 128 // pair
    lane = iota((128, 256), 1)
    source = (lane // 128) * coils + lane % coils
    for c in range(coils):
        pick = one_hot(iota((128, 256), 0) == (c % per_tile) * pair + source)
        tile = (c // per_tile) * 128
        spread = dot(taps_ref[:, tile : tile + 128], pick)
        for half in range(2):
            rows_of_coil = pl.ds(c, taps_ref.shape[0], stride=coils)
            flat[half, rows_of_coil, :] = spread[:, half * 128 : half * 128 + 128]


def write_orders(order):
    rows = order.shape[1]
    row, col = iota((rows, rows), 0), iota((rows, rows), 1)
    order[:rows] = one_hot(row == col)
    order[rows:] = one_hot(rows - 1 - row == col)


def table_kernel(size_x, flat, table, order):
    write_orders(order)
    coils = COILS
    channels = 2 * coils
    width = size_x * channels
    group = 128 // channels
    imaginary = iota((coils, 128), 1) // coils % 2 == 1
    lane_group = iota((channels, 128), 1) // channels

    def add_taps(step, carry):
        dy, dz = step // KS, step % KS
        for half in range(2):
            mats = []
            for dx in range(KS):
                tap = (dx * KS + dy) * KS + dz
                real_at = pl.multiple_of(2 * tap * coils, coils)
                imag_at = pl.multiple_of((2 * tap + 1) * coils, coils)
                real = flat[half, pl.ds(real_at, coils), :]
                imag = flat[half, pl.ds(imag_at, coils), :]
                if half == 0:
                    top = jnp.where(imaginary, -imag, real)
                    low = jnp.where(imaginary, real, imag)
                else:
                    top = jnp.where(imaginary, imag, real)
                    low = jnp.where(imaginary, -real, imag)
                mats.append(jnp.concatenate([top, low], axis=0).astype(jnp.bfloat16))
            known = {}
            zero = jnp.zeros((channels, 128), jnp.bfloat16)
            for x_out in range(size_x):
                for j in range(width // 128):
                    at = [j * group + g for g in range(group)]
                    if half == 1:
                        at = [size_x - 1 - a for a in at]
                    which = tuple(a - x_out + REACH if 0 <= a - x_out + REACH < KS else -1 for a in at)
                    if which not in known:
                        block = zero
                        for g, dx in enumerate(which):
                            if dx >= 0:
                                block = jnp.where(lane_group == g, mats[dx], block)
                        known[which] = block
                    lanes = slice(half * width + j * 128, half * width + j * 128 + 128)
                    table[dy, dz, x_out * channels : (x_out + 1) * channels, lanes] = known[which]
        return carry

    lax.fori_loop(0, table.shape[0] * KS, add_taps, 0)


def load_half(sizes, blocks_ref, order_ref, local_z, coded, points, mirrored):
    count_x, count_y, _ = sizes
    at_x, at_y = lax.axis_index(SPACE[0]), lax.axis_index(SPACE[1])
    rows = order_ref.shape[1]
    edge = REACH * local_z
    field = jnp.concatenate(
        [
            jnp.concatenate(
                [blocks_ref[(at_y ^ gy) * count_x + (at_x ^ gx)] for gy in range(count_y)], axis=1
            )
            for gx in range(count_x)
        ],
        axis=0,
    )
    both = dot_nt(order_ref[...], field)
    coded[...] = both[:rows]
    both = jnp.where(both < LIMIT, both, 0.0).astype(jnp.bfloat16)
    for ref, values in ((points, both[:rows]), (mirrored, both[rows:])):
        ref[:edge] = jnp.zeros((edge, ref.shape[1]), jnp.bfloat16)
        ref[edge + rows :] = jnp.zeros((edge, ref.shape[1]), jnp.bfloat16)
        ref[edge : edge + rows] = values


def y_taps(ref, rows, local_z, weights):
    total = None
    for dy in range(KS):
        term = dot_nt(ref[dy * local_z : dy * local_z + rows], weights(dy))
        total = term if total is None else total + term
    return total


def near_kernel(sizes, local_z, blocks_ref, order_ref, table, partial, coded, points, mirrored):
    rows, width = coded.shape
    load_half(sizes, blocks_ref, order_ref, local_z, coded, points, mirrored)
    for dz in range(KS):
        partial[0, dz] = y_taps(points, rows, local_z, lambda dy: table[dy, dz, :, :width])
        partial[1, dz] = y_taps(mirrored, rows, local_z, lambda dy: table[dy, dz, :, width:])


def shift_z(own, other, shift, local_z, dim, own_first):
    length = own.shape[dim]
    inside = iota(own.shape, dim) % local_z + shift
    inside = (inside >= 0) & (inside < local_z)
    across = pltpu.roll(other, (local_z - shift if shift > 0 else -local_z - shift) % length, dim)
    keep = own_first if shift > 0 else 1.0 - own_first
    return jnp.where(inside, pltpu.roll(own, -shift % length, dim), across * keep)


def grid_kernel(
    sizes, blocks_ref, measured_ref, mask_ref, order_ref, table, partial, coded_near,
    out_ref, coded_far, points, mirrored, near, far, lined,
):
    parts, coils, local_x, local_y, local_z = out_ref.shape
    channels = parts * coils
    rows, width = coded_far.shape
    at_x, at_y = lax.axis_index(SPACE[0]), lax.axis_index(SPACE[1])
    own_first = (1 - lax.axis_index(SPACE[2])).astype(jnp.float32)
    edge = REACH * local_z
    load_half(sizes, blocks_ref, order_ref, local_z, coded_far, points, mirrored)
    for iteration in range(ITERS - 1):
        totals = [None, None]
        for dz in sorted(range(KS), key=lambda dz: dz == REACH):
            shift = dz - REACH
            own = partial[0, dz] + y_taps(mirrored, rows, local_z, lambda dy: table[dy, dz, :, width:])
            other = partial[1, dz] + y_taps(points, rows, local_z, lambda dy: table[dy, dz, :, :width])
            if shift != 0:
                own, other = (
                    shift_z(own, other, shift, local_z, 0, own_first),
                    shift_z(other, own, shift, local_z, 0, 1.0 - own_first),
                )
            totals = [part if total is None else total + part for total, part in zip(totals, (own, other))]
        for ref, mirror_ref, coded, total in ((near, far, coded_near, totals[0]), (far, near, coded_far, totals[1])):
            values = jnp.where(coded[...] < LIMIT, coded[...], total).astype(jnp.bfloat16)
            ref[edge : edge + rows, :width] = values
            mirror_ref[edge : edge + rows, width:] = dot(order_ref[rows:], values).astype(jnp.bfloat16)
    for ref in (near, far):
        ref[:edge] = jnp.zeros((edge, 2 * width), jnp.bfloat16)
        ref[edge + rows :] = jnp.zeros((edge, 2 * width), jnp.bfloat16)

    own_rows = local_x * channels
    own_points = local_y * local_z
    start_x = pl.multiple_of(at_x * own_rows, own_rows)
    result = None
    for dy in range(KS):
        weights = jnp.concatenate([table[dy, dz, pl.ds(start_x, own_rows), :] for dz in range(KS)], axis=0)
        start = pl.multiple_of((at_y * local_y + dy) * local_z, local_z)
        window = jnp.concatenate([near[pl.ds(start, own_points), :], far[pl.ds(start, own_points), :]], axis=0)
        term = dot_nt(weights, window)
        result = term if result is None else result + term
    total = None
    for dz in range(KS):
        own = result[dz * own_rows : (dz + 1) * own_rows, :own_points]
        other = result[dz * own_rows : (dz + 1) * own_rows, own_points:]
        if dz != REACH:
            own = shift_z(own, other, dz - REACH, local_z, 1, own_first)
        total = own if total is None else total + own

    for y in range(local_y):
        piece = total if y == 0 else pltpu.roll(total, own_points - y * local_z, 1)
        lined[pl.ds(y, own_rows, stride=local_y), :] = piece
    for x in range(local_x):
        values = lined[x * channels * local_y : (x + 1) * channels * local_y, :local_z]
        values = values.reshape(parts, coils, local_y, local_z)
        sampled = (mask_ref[x] == 1)[None, None]
        values = jnp.where(sampled, measured_ref[:, :, x].astype(jnp.float32), values)
        out_ref[:, :, x] = values.astype(jnp.bfloat16)


def swap(block, axis, bit):
    count = lax.axis_size(axis)
    return lax.ppermute(block, axis, [(i, i ^ bit) for i in range(count)])


def gathered_body(measured, sample_mask, kernel):
    parts, coils, local_x, local_y, local_z = measured.shape
    sizes = tuple(lax.axis_size(axis) for axis in SPACE)
    devices = sizes[0] * sizes[1] * sizes[2]
    channels = parts * coils
    size_x, size_y, size_z = sizes[0] * local_x, sizes[1] * local_y, sizes[2] * local_z
    width = size_x * channels
    half_rows = size_y * local_z
    in_vmem = pl.BlockSpec(memory_space=pltpu.VMEM)
    in_hbm = pl.BlockSpec(memory_space=pltpu.HBM)

    def call(kernel_fn, name, out_shape, in_specs, scratch=(), outs=1, cost=2 ** 22):
        return pl.pallas_call(
            kernel_fn,
            out_shape=out_shape,
            in_specs=in_specs,
            out_specs=in_vmem if outs == 1 else (in_vmem,) * outs,
            scratch_shapes=list(scratch),
            compiler_params=pltpu.CompilerParams(vmem_limit_bytes=VMEM_LIMIT),
            cost_estimate=pl.CostEstimate(flops=0, bytes_accessed=cost, transcendentals=0),
            name=name,
        )

    packed = call(
        pack_kernel,
        "pack",
        jax.ShapeDtypeStruct((local_x * channels, local_y * local_z), jnp.bfloat16),
        [in_hbm, in_hbm],
        [
            pltpu.VMEM(measured.shape, measured.dtype),
            pltpu.VMEM(sample_mask.shape, sample_mask.dtype),
            pltpu.VMEM((local_x, channels * local_y, local_y * local_z), jnp.float32),
            pltpu.SemaphoreType.DMA((2,)),
        ],
    )(*[pltpu.with_memory_space_constraint(a, pltpu.HBM) for a in (measured, sample_mask)])

    def after(arrived, *work):
        return lax.optimization_barrier((arrived,) + work)

    taps = jnp.moveaxis(kernel, 0, 3).reshape(parts * KS ** 3, coils * 2 * coils)
    taps = jnp.pad(taps, ((0, -taps.shape[0] % 16), (0, 0)))
    steps = [(axis, 1 << bit) for axis in SPACE for bit in range(lax.axis_size(axis).bit_length() - 1)]
    blocks = packed[None]
    table, order = None, None
    for number, (axis, bit) in enumerate(steps):
        arrived = swap(blocks, axis, bit)
        if number == 0:
            arrived, taps = after(arrived, taps)
        elif number == 1:
            flat_shape = jax.ShapeDtypeStruct((2, taps.shape[0] * coils, 128), jnp.float32)
            arrived, flat = after(arrived, call(flat_kernel, "flat", flat_shape, [in_vmem])(taps))
        elif number == 2:
            table_shape = jax.ShapeDtypeStruct((KS, KS, width, 2 * width), jnp.bfloat16)
            order_shape = jax.ShapeDtypeStruct((2 * half_rows, half_rows), jnp.bfloat16)
            table_fn = functools.partial(table_kernel, size_x)
            table, order = call(table_fn, "table", (table_shape, order_shape), [in_vmem], outs=2)(flat)
            arrived, table, order = after(arrived, table, order)
        elif number == len(steps) - 1:
            padded_rows = half_rows + 2 * REACH * local_z
            padded = pltpu.VMEM((padded_rows, width), jnp.bfloat16)
            partial_shape = jax.ShapeDtypeStruct((2, KS, half_rows, width), jnp.float32)
            coded_shape = jax.ShapeDtypeStruct((half_rows, width), jnp.float32)
            partial, coded = call(
                functools.partial(near_kernel, sizes, local_z),
                "near",
                (partial_shape, coded_shape),
                [in_vmem] * 3,
                [padded, padded],
                outs=2,
            )(blocks, order, table)
            arrived, partial, coded = after(arrived, partial, coded)
            break
        blocks = jnp.concatenate([blocks, arrived], axis=0)

    both = pltpu.VMEM((padded_rows, 2 * width), jnp.bfloat16)
    return call(
        functools.partial(grid_kernel, sizes),
        "grid",
        jax.ShapeDtypeStruct(measured.shape, jnp.bfloat16),
        [in_vmem] * 7,
        [
            pltpu.VMEM((half_rows, width), jnp.float32),
            padded,
            padded,
            both,
            both,
            pltpu.VMEM((local_x * channels * local_y, 128), jnp.float32),
        ],
    )(arrived, measured, sample_mask, order, table, partial, coded)


def partner(block, axis, bit):
    count = lax.axis_size(axis)
    route = []
    for low in range(count):
        high = low | 1 << bit
        if high != low and high < count:
            route += [(low, high), (high, low)]
    return lax.ppermute(block, axis, route)


def padded_2(shard, sides, width):
    for axis, dim in sides:
        size, length = (lax.axis_size(axis), shard.shape[dim])
        up = [(i, (i + 1) % size) for i in range(size - 1)]
        down = [(j, i) for i, j in up]
        last = lax.slice_in_dim(shard, length - width, length, axis=dim)
        leading = lax.slice_in_dim(shard, 0, width, axis=dim)
        before = lax.ppermute(last, axis, up)
        after = lax.ppermute(leading, axis, down)
        shard = jnp.concatenate([before, shard, after], axis=dim)
    return shard


def unpack_kernel(kernel):
    shaped = kernel.reshape(2, KS, KS, KS, COILS, 2 * COILS)
    return jnp.transpose(shaped, (0, 4, 5, 1, 2, 3))


def tap_matrix(kernel_part):
    real_part = kernel_part[0]
    imag_part = kernel_part[1]
    upper_rows = jnp.concatenate([real_part, -imag_part], axis=1)
    lower_rows = jnp.concatenate([imag_part, real_part], axis=1)
    blocks = jnp.concatenate([upper_rows, lower_rows], axis=0)
    return jnp.transpose(blocks, (2, 3, 0, 4, 1))


def conjugate(values):
    return jnp.concatenate([values[:1], -values[1:]], axis=0)


def convolve(padded, tap_table):
    extent = tap_table.shape[0]
    channel_count = padded.shape[0] * padded.shape[1]
    channels = padded.reshape((channel_count,) + padded.shape[2:])
    size_x = channels.shape[1] - extent + 1
    size_y = channels.shape[2] - extent + 1
    size_z = channels.shape[3] - extent + 1
    out_rows = tap_table.shape[2]
    running = jnp.zeros((out_rows, size_x * size_y * size_z), jnp.float32)
    for offset_x in range(extent):
        for offset_y in range(extent):
            pieces = [
                channels[
                    :,
                    offset_x : offset_x + size_x,
                    offset_y : offset_y + size_y,
                    offset_z : offset_z + size_z,
                ]
                for offset_z in range(extent)
            ]
            stacked = jnp.stack(pieces).reshape(extent * channel_count, size_x * size_y * size_z)
            weights = tap_table[offset_x, offset_y].reshape(out_rows, extent * channel_count)
            running = running + jnp.dot(weights, stacked, preferred_element_type=jnp.float32)
    return running.reshape(2, out_rows // 2, size_x, size_y, size_z)


def mirror_state(values):
    values = values[:, :, ::-1, ::-1, ::-1]
    for bit_place in range(lax.axis_size(("gx", "gy", "gz")).bit_length() - 1):
        values = partner(values, ("gx", "gy", "gz"), bit_place)
    return values


def halo_body(measured, sample_mask, kernel):
    kernel = unpack_kernel(kernel)
    reach = kernel.shape[-1] // 2
    sampled = (sample_mask == 1)[None, None]
    current = jnp.where(sampled, measured, jnp.zeros_like(measured))
    tap_table = tap_matrix(kernel)
    for iteration in range(ITERS):
        joined = jnp.concatenate([current, conjugate(mirror_state(current))], axis=1)
        padded = padded_2(joined, (("gx", 2), ("gy", 3), ("gz", 4)), reach)
        convolved = convolve(padded, tap_table)
        current = jnp.where(sampled, measured.astype(jnp.float32), convolved).astype(jnp.bfloat16)
    return current


def solution(mesh):
    grid = tuple(mesh.shape[axis] for axis in SPACE)
    spec = P(None, "echo", "gx", "gy", "gz")

    def body(measured, sample_mask, kernel):
        parts, coils, local_x, local_y, local_z = measured.shape
        width = grid[0] * local_x * parts * coils
        points = grid[1] * local_y * local_z
        small = width == 256 and grid[1:] == (2, 2) and points == 256 and local_y * local_z == 128
        if small:
            return gathered_body(measured, sample_mask, kernel)
        return halo_body(measured, sample_mask, kernel)

    return jax.shard_map(
        body,
        mesh=mesh,
        in_specs=(spec, P(("echo", "gx"), "gy", "gz"), P()),
        out_specs=spec,
        check_vma=False,
    )
```

```python
import functools

import jax
import jax.numpy as jnp
from jax import lax
from jax.experimental import pallas as pl
from jax.experimental.pallas import tpu as pltpu
from jax.sharding import PartitionSpec as P

COILS = 16
KS = 5
REACH = KS // 2
ITERS = 2
SPACE = ("gx", "gy", "gz")
UNSAMPLED = 2.0 ** 100
LIMIT = 2.0 ** 99
VMEM_LIMIT = 16 * 2 ** 20


def iota(shape, dim):
    return lax.broadcasted_iota(jnp.int32, shape, dim)


def one_hot(flags):
    return jnp.where(flags, 1.0, 0.0).astype(jnp.bfloat16)


def dot(a, b):
    return jnp.dot(a, b, preferred_element_type=jnp.float32)


def dot_nt(a, b):
    return lax.dot_general(a, b, (((1,), (1,)), ((), ())), preferred_element_type=jnp.float32)


def pack_kernel(measured_hbm, mask_hbm, packed_ref, measured_ref, mask_ref, lined, sems):
    copies = [
        pltpu.make_async_copy(measured_hbm, measured_ref, sems.at[0]),
        pltpu.make_async_copy(mask_hbm, mask_ref, sems.at[1]),
    ]
    for copy in copies:
        copy.start()
    for copy in copies:
        copy.wait()
    parts, coils, size_x, size_y, size_z = measured_ref.shape
    channels = parts * coils
    rows = channels * size_y
    for x in range(size_x):
        values = measured_ref[:, :, x].astype(jnp.float32)
        sampled = (mask_ref[x] == 1)[None, None]
        lined[x, :, :size_z] = jnp.where(sampled, values, UNSAMPLED).reshape(rows, size_z)
    lane_y = iota((channels, size_y * size_z), 1) // size_z
    for x in range(size_x):
        packed = None
        for y in range(size_y):
            piece = lined[x, pl.ds(y, channels, stride=size_y), :]
            if y > 0:
                piece = jnp.where(lane_y == y, pltpu.roll(piece, y * size_z, 1), packed)
            packed = piece
        packed_ref[x * channels : (x + 1) * channels] = packed.astype(jnp.bfloat16)


def flat_kernel(taps_ref, flat):
    coils = COILS
    pair = 2 * coils
    per_tile = 128 // pair
    lane = iota((128, 256), 1)
    source = (lane // 128) * coils + lane % coils
    for c in range(coils):
        pick = one_hot(iota((128, 256), 0) == (c % per_tile) * pair + source)
        tile = (c // per_tile) * 128
        spread = dot(taps_ref[:, tile : tile + 128], pick)
        for half in range(2):
            rows_of_coil = pl.ds(c, taps_ref.shape[0], stride=coils)
            flat[half, rows_of_coil, :] = spread[:, half * 128 : half * 128 + 128]


def write_orders(order):
    rows = order.shape[1]
    row, col = iota((rows, rows), 0), iota((rows, rows), 1)
    order[:rows] = one_hot(row == col)
    order[rows:] = one_hot(rows - 1 - row == col)


def table_kernel(size_x, flat, table, mirror):
    rows = mirror.shape[0]
    mirror[...] = one_hot(rows - 1 - iota((rows, rows), 0) == iota((rows, rows), 1))
    coils = COILS
    channels = 2 * coils
    width = size_x * channels
    group = 128 // channels
    imaginary = iota((coils, 128), 1) // coils % 2 == 1
    lane_group = iota((channels, 128), 1) // channels

    def add_taps(step, carry):
        dy, dz = step // KS, step % KS
        for half in range(2):
            mats = []
            for dx in range(KS):
                tap = (dx * KS + dy) * KS + dz
                real_at = pl.multiple_of(2 * tap * coils, coils)
                imag_at = pl.multiple_of((2 * tap + 1) * coils, coils)
                real = flat[half, pl.ds(real_at, coils), :]
                imag = flat[half, pl.ds(imag_at, coils), :]
                if half == 0:
                    top = jnp.where(imaginary, -imag, real)
                    low = jnp.where(imaginary, real, imag)
                else:
                    top = jnp.where(imaginary, imag, real)
                    low = jnp.where(imaginary, -real, imag)
                mats.append(jnp.concatenate([top, low], axis=0).astype(jnp.bfloat16))
            known = {}
            zero = jnp.zeros((channels, 128), jnp.bfloat16)
            for x_out in range(size_x):
                for j in range(width // 128):
                    at = [j * group + g for g in range(group)]
                    if half == 1:
                        at = [size_x - 1 - a for a in at]
                    which = tuple(a - x_out + REACH if 0 <= a - x_out + REACH < KS else -1 for a in at)
                    if which not in known:
                        block = zero
                        for g, dx in enumerate(which):
                            if dx >= 0:
                                block = jnp.where(lane_group == g, mats[dx], block)
                        known[which] = block
                    lanes = slice(half * width + j * 128, half * width + j * 128 + 128)
                    table[dy, dz, x_out * channels : (x_out + 1) * channels, lanes] = known[which]
        return carry

    lax.fori_loop(0, table.shape[0] * KS, add_taps, 0)


def turn(blocks_ref, order):
    count_x = blocks_ref.shape[0]
    at_x = lax.axis_index(SPACE[0])
    field = jnp.concatenate([blocks_ref[at_x ^ gx] for gx in range(count_x)], axis=0)
    return dot_nt(order, field).astype(jnp.bfloat16)


def turn_kernel(blocks_ref, turned, order):
    write_orders(order)
    turned[...] = turn(blocks_ref, order[...])


def join_kernel(blocks_ref, turned, order, half):
    other = turn(blocks_ref, order[...])
    quarter = order.shape[1]
    rows = 2 * quarter
    at_y = lax.axis_index(SPACE[1])
    for values, place in ((turned[...], at_y), (other, 1 - at_y)):
        start = pl.multiple_of(place * quarter, quarter)
        half[pl.ds(start, quarter)] = values[:quarter]
        start = pl.multiple_of(rows + (1 - place) * quarter, quarter)
        half[pl.ds(start, quarter)] = values[quarter:]


def load_half(half, local_z, points, mirrored):
    rows, width = half.shape[0] // 2, half.shape[1]
    edge = REACH * local_z
    for number, ref in enumerate((points, mirrored)):
        values = half[number * rows : (number + 1) * rows]
        ref[:edge] = jnp.zeros((edge, width), jnp.bfloat16)
        ref[edge + rows :] = jnp.zeros((edge, width), jnp.bfloat16)
        ref[edge : edge + rows] = jnp.where(values < LIMIT, values, jnp.zeros_like(values))


def y_taps(ref, rows, local_z, weights):
    total = None
    for dy in range(KS):
        term = dot_nt(ref[dy * local_z : dy * local_z + rows], weights(dy))
        total = term if total is None else total + term
    return total


def near_kernel(local_z, half, table, partial, points, mirrored):
    rows, width = half.shape[0] // 2, half.shape[1]
    load_half(half, local_z, points, mirrored)
    for dz in range(KS):
        partial[0, dz] = y_taps(points, rows, local_z, lambda dy: table[dy, dz, :, :width])
        partial[1, dz] = y_taps(mirrored, rows, local_z, lambda dy: table[dy, dz, :, width:])


def shift_z(own, other, shift, local_z, dim, own_first):
    length = own.shape[dim]
    inside = iota(own.shape, dim) % local_z + shift
    inside = (inside >= 0) & (inside < local_z)
    across = pltpu.roll(other, (local_z - shift if shift > 0 else -local_z - shift) % length, dim)
    keep = own_first if shift > 0 else 1.0 - own_first
    return jnp.where(inside, pltpu.roll(own, -shift % length, dim), across * keep)


def grid_kernel(
    half_near, half_far, measured_ref, mask_ref, mirror, table, partial,
    out_ref, points, mirrored, near, far, lined,
):
    parts, coils, local_x, local_y, local_z = out_ref.shape
    channels = parts * coils
    rows, width = half_near.shape[0] // 2, half_near.shape[1]
    at_x, at_y = lax.axis_index(SPACE[0]), lax.axis_index(SPACE[1])
    own_first = (1 - lax.axis_index(SPACE[2])).astype(jnp.float32)
    edge = REACH * local_z
    load_half(half_far, local_z, points, mirrored)
    for iteration in range(ITERS - 1):
        totals = [None, None]
        for dz in sorted(range(KS), key=lambda dz: dz == REACH):
            shift = dz - REACH
            own = partial[0, dz] + y_taps(mirrored, rows, local_z, lambda dy: table[dy, dz, :, width:])
            other = partial[1, dz] + y_taps(points, rows, local_z, lambda dy: table[dy, dz, :, :width])
            if shift != 0:
                own, other = (
                    shift_z(own, other, shift, local_z, 0, own_first),
                    shift_z(other, own, shift, local_z, 0, 1.0 - own_first),
                )
            totals = [part if total is None else total + part for total, part in zip(totals, (own, other))]
        for ref, mirror_ref, coded, total in ((near, far, half_near, totals[0]), (far, near, half_far, totals[1])):
            coded = coded[:rows]
            values = jnp.where(coded < LIMIT, coded, total.astype(jnp.bfloat16))
            ref[edge : edge + rows, :width] = values
            mirror_ref[edge : edge + rows, width:] = dot(mirror[...], values).astype(jnp.bfloat16)
    for ref in (near, far):
        ref[:edge] = jnp.zeros((edge, 2 * width), jnp.bfloat16)
        ref[edge + rows :] = jnp.zeros((edge, 2 * width), jnp.bfloat16)

    own_rows = local_x * channels
    own_points = local_y * local_z
    start_x = pl.multiple_of(at_x * own_rows, own_rows)
    result = None
    for dy in range(KS):
        weights = jnp.concatenate([table[dy, dz, pl.ds(start_x, own_rows), :] for dz in range(KS)], axis=0)
        start = pl.multiple_of((at_y * local_y + dy) * local_z, local_z)
        window = jnp.concatenate([near[pl.ds(start, own_points), :], far[pl.ds(start, own_points), :]], axis=0)
        term = dot_nt(weights, window)
        result = term if result is None else result + term
    total = None
    for dz in range(KS):
        own = result[dz * own_rows : (dz + 1) * own_rows, :own_points]
        other = result[dz * own_rows : (dz + 1) * own_rows, own_points:]
        if dz != REACH:
            own = shift_z(own, other, dz - REACH, local_z, 1, own_first)
        total = own if total is None else total + own

    for y in range(local_y):
        piece = total if y == 0 else pltpu.roll(total, own_points - y * local_z, 1)
        lined[pl.ds(y, own_rows, stride=local_y), :] = piece
    for x in range(local_x):
        values = lined[x * channels * local_y : (x + 1) * channels * local_y, :local_z]
        values = values.reshape(parts, coils, local_y, local_z)
        sampled = (mask_ref[x] == 1)[None, None]
        values = jnp.where(sampled, measured_ref[:, :, x].astype(jnp.float32), values)
        out_ref[:, :, x] = values.astype(jnp.bfloat16)


def swap(block, axis, bit):
    count = lax.axis_size(axis)
    return lax.ppermute(block, axis, [(i, i ^ bit) for i in range(count)])


def gathered_body(measured, sample_mask, kernel):
    parts, coils, local_x, local_y, local_z = measured.shape
    sizes = tuple(lax.axis_size(axis) for axis in SPACE)
    devices = sizes[0] * sizes[1] * sizes[2]
    channels = parts * coils
    size_x, size_y, size_z = sizes[0] * local_x, sizes[1] * local_y, sizes[2] * local_z
    width = size_x * channels
    half_rows = size_y * local_z
    in_vmem = pl.BlockSpec(memory_space=pltpu.VMEM)
    in_hbm = pl.BlockSpec(memory_space=pltpu.HBM)

    def call(kernel_fn, name, out_shape, in_specs, scratch=(), outs=1, cost=2 ** 22):
        return pl.pallas_call(
            kernel_fn,
            out_shape=out_shape,
            in_specs=in_specs,
            out_specs=in_vmem if outs == 1 else (in_vmem,) * outs,
            scratch_shapes=list(scratch),
            compiler_params=pltpu.CompilerParams(vmem_limit_bytes=VMEM_LIMIT),
            cost_estimate=pl.CostEstimate(flops=0, bytes_accessed=cost, transcendentals=0),
            name=name,
        )

    packed = call(
        pack_kernel,
        "pack",
        jax.ShapeDtypeStruct((local_x * channels, local_y * local_z), jnp.bfloat16),
        [in_hbm, in_hbm],
        [
            pltpu.VMEM(measured.shape, measured.dtype),
            pltpu.VMEM(sample_mask.shape, sample_mask.dtype),
            pltpu.VMEM((local_x, channels * local_y, local_y * local_z), jnp.float32),
            pltpu.SemaphoreType.DMA((2,)),
        ],
    )(*[pltpu.with_memory_space_constraint(a, pltpu.HBM) for a in (measured, sample_mask)])

    def after(arrived, *work):
        return lax.optimization_barrier((arrived,) + work)

    taps = jnp.moveaxis(kernel, 0, 3).reshape(parts * KS ** 3, coils * 2 * coils)
    taps = jnp.pad(taps, ((0, -taps.shape[0] % 16), (0, 0)))
    steps = [(axis, 1 << bit) for axis in SPACE for bit in range(lax.axis_size(axis).bit_length() - 1)]
    blocks = packed[None]
    for number, (axis, bit) in enumerate(steps):
        arrived = swap(blocks, axis, bit)
        if number == 0:
            arrived, taps = after(arrived, taps)
        elif number == 1:
            flat_shape = jax.ShapeDtypeStruct((2, taps.shape[0] * coils, 128), jnp.float32)
            arrived, flat = after(arrived, call(flat_kernel, "flat", flat_shape, [in_vmem])(taps))
        elif number == 2:
            table_shape = jax.ShapeDtypeStruct((KS, KS, width, 2 * width), jnp.bfloat16)
            mirror_shape = jax.ShapeDtypeStruct((half_rows, half_rows), jnp.bfloat16)
            table_fn = functools.partial(table_kernel, size_x)
            table, mirror = call(table_fn, "table", (table_shape, mirror_shape), [in_vmem], outs=2)(flat)
            turned_shape = jax.ShapeDtypeStruct((half_rows, width), jnp.bfloat16)
            order_shape = jax.ShapeDtypeStruct((half_rows, half_rows // 2), jnp.bfloat16)
            turned, order = call(turn_kernel, "turn", (turned_shape, order_shape), [in_vmem], outs=2)(blocks)
            arrived, table, mirror, turned, order = after(arrived, table, mirror, turned, order)
            half_shape = jax.ShapeDtypeStruct((2 * half_rows, width), jnp.bfloat16)
            blocks = call(join_kernel, "join", half_shape, [in_vmem] * 3)(arrived, turned, order)
            continue
        elif number == len(steps) - 1:
            padded_rows = half_rows + 2 * REACH * local_z
            padded = pltpu.VMEM((padded_rows, width), jnp.bfloat16)
            partial_shape = jax.ShapeDtypeStruct((2, KS, half_rows, width), jnp.float32)
            near_fn = functools.partial(near_kernel, local_z)
            partial = call(near_fn, "near", partial_shape, [in_vmem] * 2, [padded, padded])(blocks, table)
            arrived, partial = after(arrived, partial)
            break
        blocks = jnp.concatenate([blocks, arrived], axis=0)

    both = pltpu.VMEM((padded_rows, 2 * width), jnp.bfloat16)
    lined = pltpu.VMEM((local_x * channels * local_y, 128), jnp.float32)
    return call(
        grid_kernel,
        "grid",
        jax.ShapeDtypeStruct(measured.shape, jnp.bfloat16),
        [in_vmem] * 7,
        [padded, padded, both, both, lined],
    )(blocks, arrived, measured, sample_mask, mirror, table, partial)


def partner(block, axis, bit):
    count = lax.axis_size(axis)
    route = []
    for low in range(count):
        high = low | 1 << bit
        if high != low and high < count:
            route += [(low, high), (high, low)]
    return lax.ppermute(block, axis, route)


def padded_2(shard, sides, width):
    for axis, dim in sides:
        size, length = (lax.axis_size(axis), shard.shape[dim])
        up = [(i, (i + 1) % size) for i in range(size - 1)]
        down = [(j, i) for i, j in up]
        last = lax.slice_in_dim(shard, length - width, length, axis=dim)
        leading = lax.slice_in_dim(shard, 0, width, axis=dim)
        before = lax.ppermute(last, axis, up)
        after = lax.ppermute(leading, axis, down)
        shard = jnp.concatenate([before, shard, after], axis=dim)
    return shard


def unpack_kernel(kernel):
    shaped = kernel.reshape(2, KS, KS, KS, COILS, 2 * COILS)
    return jnp.transpose(shaped, (0, 4, 5, 1, 2, 3))


def tap_matrix(kernel_part):
    real_part = kernel_part[0]
    imag_part = kernel_part[1]
    upper_rows = jnp.concatenate([real_part, -imag_part], axis=1)
    lower_rows = jnp.concatenate([imag_part, real_part], axis=1)
    blocks = jnp.concatenate([upper_rows, lower_rows], axis=0)
    return jnp.transpose(blocks, (2, 3, 0, 4, 1))


def conjugate(values):
    return jnp.concatenate([values[:1], -values[1:]], axis=0)


def convolve(padded, tap_table):
    extent = tap_table.shape[0]
    channel_count = padded.shape[0] * padded.shape[1]
    channels = padded.reshape((channel_count,) + padded.shape[2:])
    size_x = channels.shape[1] - extent + 1
    size_y = channels.shape[2] - extent + 1
    size_z = channels.shape[3] - extent + 1
    out_rows = tap_table.shape[2]
    running = jnp.zeros((out_rows, size_x * size_y * size_z), jnp.float32)
    for offset_x in range(extent):
        for offset_y in range(extent):
            pieces = [
                channels[
                    :,
                    offset_x : offset_x + size_x,
                    offset_y : offset_y + size_y,
                    offset_z : offset_z + size_z,
                ]
                for offset_z in range(extent)
            ]
            stacked = jnp.stack(pieces).reshape(extent * channel_count, size_x * size_y * size_z)
            weights = tap_table[offset_x, offset_y].reshape(out_rows, extent * channel_count)
            running = running + jnp.dot(weights, stacked, preferred_element_type=jnp.float32)
    return running.reshape(2, out_rows // 2, size_x, size_y, size_z)


def mirror_state(values):
    values = values[:, :, ::-1, ::-1, ::-1]
    for bit_place in range(lax.axis_size(("gx", "gy", "gz")).bit_length() - 1):
        values = partner(values, ("gx", "gy", "gz"), bit_place)
    return values


def halo_body(measured, sample_mask, kernel):
    kernel = unpack_kernel(kernel)
    reach = kernel.shape[-1] // 2
    sampled = (sample_mask == 1)[None, None]
    current = jnp.where(sampled, measured, jnp.zeros_like(measured))
    tap_table = tap_matrix(kernel)
    for iteration in range(ITERS):
        joined = jnp.concatenate([current, conjugate(mirror_state(current))], axis=1)
        padded = padded_2(joined, (("gx", 2), ("gy", 3), ("gz", 4)), reach)
        convolved = convolve(padded, tap_table)
        current = jnp.where(sampled, measured.astype(jnp.float32), convolved).astype(jnp.bfloat16)
    return current


def solution(mesh):
    grid = tuple(mesh.shape[axis] for axis in SPACE)
    spec = P(None, "echo", "gx", "gy", "gz")

    def body(measured, sample_mask, kernel):
        parts, coils, local_x, local_y, local_z = measured.shape
        width = grid[0] * local_x * parts * coils
        points = grid[1] * local_y * local_z
        small = width == 256 and grid[1:] == (2, 2) and points == 256 and local_y * local_z == 128
        if small:
            return gathered_body(measured, sample_mask, kernel)
        return halo_body(measured, sample_mask, kernel)

    return jax.shard_map(
        body,
        mesh=mesh,
        in_specs=(spec, P(("echo", "gx"), "gy", "gz"), P()),
        out_specs=spec,
        check_vma=False,
    )
```

```python
import functools

import jax
import jax.numpy as jnp
from jax import lax
from jax.experimental import pallas as pl
from jax.experimental.pallas import tpu as pltpu
from jax.sharding import PartitionSpec as P

COILS = 16
KS = 5
NEAR = 3
REACH = KS // 2
ITERS = 2
SPACE = ("gx", "gy", "gz")
UNSAMPLED = 2.0 ** 100
LIMIT = 2.0 ** 99
VMEM_LIMIT = 16 * 2 ** 20


def iota(shape, dim):
    return lax.broadcasted_iota(jnp.int32, shape, dim)


def one_hot(flags):
    return jnp.where(flags, 1.0, 0.0).astype(jnp.bfloat16)


def dot(a, b):
    return jnp.dot(a, b, preferred_element_type=jnp.float32)


def dot_nt(a, b):
    return lax.dot_general(a, b, (((1,), (1,)), ((), ())), preferred_element_type=jnp.float32)


def pack_kernel(measured_hbm, mask_hbm, packed_ref, measured_ref, mask_ref, lined, sems):
    copies = [
        pltpu.make_async_copy(measured_hbm, measured_ref, sems.at[0]),
        pltpu.make_async_copy(mask_hbm, mask_ref, sems.at[1]),
    ]
    for copy in copies:
        copy.start()
    for copy in copies:
        copy.wait()
    parts, coils, size_x, size_y, size_z = measured_ref.shape
    channels = parts * coils
    rows = channels * size_y
    for x in range(size_x):
        values = measured_ref[:, :, x].astype(jnp.float32)
        sampled = (mask_ref[x] == 1)[None, None]
        lined[x, :, :size_z] = jnp.where(sampled, values, UNSAMPLED).reshape(rows, size_z)
    lane_y = iota((channels, size_y * size_z), 1) // size_z
    for x in range(size_x):
        packed = None
        for y in range(size_y):
            piece = lined[x, pl.ds(y, channels, stride=size_y), :]
            if y > 0:
                piece = jnp.where(lane_y == y, pltpu.roll(piece, y * size_z, 1), packed)
            packed = piece
        packed_ref[x * channels : (x + 1) * channels] = packed.astype(jnp.bfloat16)


def flat_kernel(taps_ref, flat):
    coils = COILS
    pair = 2 * coils
    per_tile = 128 // pair
    lane = iota((128, 256), 1)
    source = (lane // 128) * coils + lane % coils
    for c in range(coils):
        pick = one_hot(iota((128, 256), 0) == (c % per_tile) * pair + source)
        tile = (c // per_tile) * 128
        spread = dot(taps_ref[:, tile : tile + 128], pick)
        for half in range(2):
            rows_of_coil = pl.ds(c, taps_ref.shape[0], stride=coils)
            flat[half, rows_of_coil, :] = spread[:, half * 128 : half * 128 + 128]


def write_orders(order):
    rows = order.shape[1]
    row, col = iota((rows, rows), 0), iota((rows, rows), 1)
    order[:rows] = one_hot(row == col)
    order[rows:] = one_hot(rows - 1 - row == col)


def table_kernel(order_x, flat, table):
    size_x = len(order_x)
    coils = COILS
    channels = 2 * coils
    width = size_x * channels
    group = 128 // channels
    imaginary = iota((coils, 128), 1) // coils % 2 == 1
    lane_group = iota((channels, 128), 1) // channels

    def add_taps(step, carry):
        dy, dz = step // KS, step % KS
        for half in range(2):
            mats = []
            for dx in range(KS):
                tap = (dx * KS + dy) * KS + dz
                real_at = pl.multiple_of(2 * tap * coils, coils)
                imag_at = pl.multiple_of((2 * tap + 1) * coils, coils)
                real = flat[half, pl.ds(real_at, coils), :]
                imag = flat[half, pl.ds(imag_at, coils), :]
                if half == 0:
                    top = jnp.where(imaginary, -imag, real)
                    low = jnp.where(imaginary, real, imag)
                else:
                    top = jnp.where(imaginary, imag, real)
                    low = jnp.where(imaginary, -real, imag)
                mats.append(jnp.concatenate([top, low], axis=0).astype(jnp.bfloat16))
            known = {}
            zero = jnp.zeros((channels, 128), jnp.bfloat16)
            for row, x_out in enumerate(order_x):
                for j in range(width // 128):
                    at = order_x[j * group : (j + 1) * group]
                    if half == 1:
                        at = [size_x - 1 - a for a in at]
                    which = tuple(a - x_out + REACH if 0 <= a - x_out + REACH < KS else -1 for a in at)
                    if which not in known:
                        block = zero
                        for g, dx in enumerate(which):
                            if dx >= 0:
                                block = jnp.where(lane_group == g, mats[dx], block)
                        known[which] = block
                    lanes = slice(half * width + j * 128, half * width + j * 128 + 128)
                    table[dy, dz, row * channels : (row + 1) * channels, lanes] = known[which]
        return carry

    lax.fori_loop(0, table.shape[0] * KS, add_taps, 0)


def turn(blocks_ref, order, count_x, count_y):
    at_x, at_y = lax.axis_index(SPACE[0]) // 2, lax.axis_index(SPACE[1])
    field = jnp.concatenate(
        [
            jnp.concatenate([blocks_ref[(at_y ^ gy) * count_x + (at_x ^ gx)] for gy in range(count_y)], axis=1)
            for gx in range(count_x)
        ],
        axis=0,
    )
    return dot_nt(order, field).astype(jnp.bfloat16)


def turn_kernel(count_x, count_y, blocks_ref, order, turned):
    turned[...] = turn(blocks_ref, order[...], count_x, count_y)


def join_kernel(count_x, count_y, blocks_ref, turned, order, half):
    other = turn(blocks_ref, order[...], count_x, count_y)
    width = turned.shape[1]
    own_part = lax.axis_index(SPACE[0]) % 2
    for values, part in ((turned[...], own_part), (other, 1 - own_part)):
        half[:, pl.ds(pl.multiple_of(part * width, width), width)] = values


def load_half(half, local_z, points, mirrored):
    rows, width = half.shape[0] // 2, half.shape[1]
    edge = REACH * local_z
    for number, ref in enumerate((points, mirrored)):
        values = half[number * rows : (number + 1) * rows]
        ref[:edge] = jnp.zeros((edge, width), jnp.bfloat16)
        ref[edge + rows :] = jnp.zeros((edge, width), jnp.bfloat16)
        ref[edge : edge + rows] = jnp.where(values < LIMIT, values, jnp.zeros_like(values))


def y_taps(ref, rows, local_z, weights):
    total = None
    for dy in range(KS):
        term = dot_nt(ref[dy * local_z : dy * local_z + rows], weights(dy))
        total = term if total is None else total + term
    return total


def pair_taps(ref, rows, local_z, weights):
    total = None
    for dy in range(0, KS, 2):
        both = range(dy, min(dy + 2, KS))
        values = jnp.concatenate([ref[d * local_z : d * local_z + rows] for d in both], axis=1)
        term = dot_nt(values, jnp.concatenate([weights(d) for d in both], axis=1))
        total = term if total is None else total + term
    return total


def near_kernel(count_x, local_z, turned, table, partial, points, mirrored):
    rows, width = turned.shape[0] // 2, turned.shape[1]
    load_half(turned, local_z, points, mirrored)
    first = lax.axis_index(SPACE[0]) % 2 * width
    for number, ref in enumerate((points, mirrored)):
        lanes = pl.ds(pl.multiple_of(number * table.shape[3] // 2 + first, width), width)
        for dz in range(NEAR):
            partial[number, dz] = pair_taps(ref, rows, local_z, lambda dy: table[dy, dz, :, lanes])


def rest_kernel(count_x, local_z, half, table, before, partial, points, mirrored, points_x, mirrored_x):
    rows, width = half.shape[0] // 2, half.shape[1]
    part = width // 2
    first = pl.multiple_of((1 - lax.axis_index(SPACE[0]) % 2) * part, part)
    load_half(half, local_z, points, mirrored)
    load_half(half.at[:, pl.ds(first, part)], local_z, points_x, mirrored_x)
    for number, (ref, ref_x) in enumerate(((points, points_x), (mirrored, mirrored_x))):
        every = slice(number * width, (number + 1) * width)
        lanes = pl.ds(pl.multiple_of(number * width + first, part), part)
        for dz in range(NEAR):
            partial[number, dz] = before[number, dz] + pair_taps(
                ref_x, rows, local_z, lambda dy: table[dy, dz, :, lanes]
            )
        for dz in range(NEAR, KS):
            partial[number, dz] = y_taps(ref, rows, local_z, lambda dy: table[dy, dz, :, every])


def shift_z(own, other, shift, local_z, dim, own_first):
    length = own.shape[dim]
    inside = iota(own.shape, dim) % local_z + shift
    inside = (inside >= 0) & (inside < local_z)
    across = pltpu.roll(other, (local_z - shift if shift > 0 else -local_z - shift) % length, dim)
    keep = own_first if shift > 0 else 1.0 - own_first
    return jnp.where(inside, pltpu.roll(own, -shift % length, dim), across * keep)


def grid_kernel(
    half_near, half_far, measured_ref, mask_ref, order, table, partial,
    out_ref, points, mirrored, near, far, near_mirrored, far_mirrored, lined,
):
    parts, coils, local_x, local_y, local_z = out_ref.shape
    channels = parts * coils
    rows, width = half_near.shape[0] // 2, half_near.shape[1]
    at_x, at_y = lax.axis_index(SPACE[0]), lax.axis_index(SPACE[1])
    at_x = at_x % 2 * (lax.axis_size(SPACE[0]) // 2) + at_x // 2
    own_first = (1 - lax.axis_index(SPACE[2])).astype(jnp.float32)
    edge = REACH * local_z
    load_half(half_far, local_z, points, mirrored)
    for ref in (near, far, near_mirrored, far_mirrored):
        ref[:edge] = jnp.zeros((edge, width), jnp.bfloat16)
        ref[edge + rows :] = jnp.zeros((edge, width), jnp.bfloat16)
    for iteration in range(ITERS - 1):
        totals = [None, None]
        for dz in sorted(range(KS), key=lambda dz: dz == REACH):
            shift = dz - REACH
            own = partial[0, dz] + y_taps(mirrored, rows, local_z, lambda dy: table[dy, dz, :, width:])
            other = partial[1, dz] + y_taps(points, rows, local_z, lambda dy: table[dy, dz, :, :width])
            if shift != 0:
                own, other = (
                    shift_z(own, other, shift, local_z, 0, own_first),
                    shift_z(other, own, shift, local_z, 0, 1.0 - own_first),
                )
            totals = [part if total is None else total + part for total, part in zip(totals, (own, other))]
        halves = ((near, far_mirrored, half_near, totals[0]), (far, near_mirrored, half_far, totals[1]))
        for ref, mirror_ref, coded, total in halves:
            coded = coded[:rows]
            values = jnp.where(coded < LIMIT, coded, total.astype(jnp.bfloat16))
            ref[edge : edge + rows] = values
            mirror_ref[edge : edge + rows] = dot(order[rows:], values).astype(jnp.bfloat16)

    own_rows = local_x * channels
    own_points = local_y * local_z
    start_x = pl.multiple_of(at_x * own_rows, own_rows)
    result = None
    for first, refs in ((0, (near, far)), (width, (near_mirrored, far_mirrored))):
        for dy in range(KS):
            taps = [table[dy, dz, pl.ds(start_x, own_rows), first : first + width] for dz in range(KS)]
            start = pl.multiple_of((at_y * local_y + dy) * local_z, local_z)
            window = jnp.concatenate([ref[pl.ds(start, own_points), :] for ref in refs], axis=0)
            term = dot_nt(jnp.concatenate(taps, axis=0), window)
            result = term if result is None else result + term
    total = None
    for dz in range(KS):
        own = result[dz * own_rows : (dz + 1) * own_rows, :own_points]
        other = result[dz * own_rows : (dz + 1) * own_rows, own_points:]
        if dz != REACH:
            own = shift_z(own, other, dz - REACH, local_z, 1, own_first)
        total = own if total is None else total + own

    for y in range(local_y):
        piece = total if y == 0 else pltpu.roll(total, own_points - y * local_z, 1)
        lined[pl.ds(y, own_rows, stride=local_y), :] = piece
    for x in range(local_x):
        values = lined[x * channels * local_y : (x + 1) * channels * local_y, :local_z]
        values = values.reshape(parts, coils, local_y, local_z)
        sampled = (mask_ref[x] == 1)[None, None]
        values = jnp.where(sampled, measured_ref[:, :, x].astype(jnp.float32), values)
        out_ref[:, :, x] = values.astype(jnp.bfloat16)


def swap(block, axis, bit):
    count = lax.axis_size(axis)
    return lax.ppermute(block, axis, [(i, i ^ bit) for i in range(count)])


def gathered_body(measured, sample_mask, kernel):
    parts, coils, local_x, local_y, local_z = measured.shape
    sizes = tuple(lax.axis_size(axis) for axis in SPACE)
    devices = sizes[0] * sizes[1] * sizes[2]
    channels = parts * coils
    size_x, size_y, size_z = sizes[0] * local_x, sizes[1] * local_y, sizes[2] * local_z
    width = size_x * channels
    half_rows = size_y * local_z
    in_vmem = pl.BlockSpec(memory_space=pltpu.VMEM)
    in_hbm = pl.BlockSpec(memory_space=pltpu.HBM)

    def call(kernel_fn, name, out_shape, in_specs, scratch=(), outs=1, cost=2 ** 22):
        return pl.pallas_call(
            kernel_fn,
            out_shape=out_shape,
            in_specs=in_specs,
            out_specs=in_vmem if outs == 1 else (in_vmem,) * outs,
            scratch_shapes=list(scratch),
            compiler_params=pltpu.CompilerParams(vmem_limit_bytes=VMEM_LIMIT),
            cost_estimate=pl.CostEstimate(flops=0, bytes_accessed=cost, transcendentals=0),
            name=name,
        )

    packed = call(
        pack_kernel,
        "pack",
        jax.ShapeDtypeStruct((local_x * channels, local_y * local_z), jnp.bfloat16),
        [in_hbm, in_hbm],
        [
            pltpu.VMEM(measured.shape, measured.dtype),
            pltpu.VMEM(sample_mask.shape, sample_mask.dtype),
            pltpu.VMEM((local_x, channels * local_y, local_y * local_z), jnp.float32),
            pltpu.SemaphoreType.DMA((2,)),
        ],
    )(*[pltpu.with_memory_space_constraint(a, pltpu.HBM) for a in (measured, sample_mask)])

    def after(arrived, *work):
        return lax.optimization_barrier((arrived,) + work)

    taps = jnp.moveaxis(kernel, 0, 3).reshape(parts * KS ** 3, coils * 2 * coils)
    taps = jnp.pad(taps, ((0, -taps.shape[0] % 16), (0, 0)))
    bits = [[(axis, 1 << bit) for bit in range(lax.axis_size(axis).bit_length() - 1)] for axis in SPACE]
    steps = bits[0][1:] + bits[1] + bits[0][:1] + bits[2]
    order_x = [gx * local_x + x for odd in range(2) for gx in range(odd, sizes[0], 2) for x in range(local_x)]
    half_x = sizes[0] // 2
    padded_rows = half_rows + 2 * REACH * local_z
    padded_part = pltpu.VMEM((padded_rows, width // 2), jnp.bfloat16)
    padded = pltpu.VMEM((padded_rows, width), jnp.bfloat16)
    partial_shape = jax.ShapeDtypeStruct((2, KS, half_rows, width), jnp.float32)
    near_shape = jax.ShapeDtypeStruct((2, NEAR, half_rows, width), jnp.float32)
    scratch = [padded, padded, padded_part, padded_part]
    blocks = packed[None]
    for number, (axis, bit) in enumerate(steps):
        arrived = swap(blocks, axis, bit)
        if number == 0:
            arrived, taps = after(arrived, taps)
        elif number == 1:
            flat_shape = jax.ShapeDtypeStruct((2, taps.shape[0] * coils, 128), jnp.float32)
            order_shape = jax.ShapeDtypeStruct((2 * half_rows, half_rows), jnp.bfloat16)
            order = call(write_orders, "order", order_shape, [])()
            flat = call(flat_kernel, "flat", flat_shape, [in_vmem])(taps)
            arrived, flat, order = after(arrived, flat, order)
        elif number == 2:
            table_shape = jax.ShapeDtypeStruct((KS, KS, width, 2 * width), jnp.bfloat16)
            table = call(functools.partial(table_kernel, order_x), "table", table_shape, [in_vmem])(flat)
            turned_shape = jax.ShapeDtypeStruct((2 * half_rows, width // 2), jnp.bfloat16)
            turn_fn = functools.partial(turn_kernel, half_x, sizes[1])
            turned = call(turn_fn, "turn", turned_shape, [in_vmem] * 2)(blocks, order)
            near_fn = functools.partial(near_kernel, half_x, local_z)
            partial = call(near_fn, "near", near_shape, [in_vmem] * 2, [padded_part] * 2)(turned, table)
            arrived, table, turned, partial = after(arrived, table, turned, partial)
            half_shape = jax.ShapeDtypeStruct((2 * half_rows, width), jnp.bfloat16)
            join_fn = functools.partial(join_kernel, half_x, sizes[1])
            blocks = call(join_fn, "join", half_shape, [in_vmem] * 3)(arrived, turned, order)
            continue
        elif number == 3:
            rest_fn = functools.partial(rest_kernel, half_x, local_z)
            partial = call(rest_fn, "rest", partial_shape, [in_vmem] * 3, scratch)(blocks, table, partial)
            arrived, partial = after(arrived, partial)
            break
        blocks = jnp.concatenate([blocks, arrived], axis=0)

    lined = pltpu.VMEM((local_x * channels * local_y, 128), jnp.float32)
    return call(
        grid_kernel,
        "grid",
        jax.ShapeDtypeStruct(measured.shape, jnp.bfloat16),
        [in_vmem] * 7,
        [padded] * 6 + [lined],
    )(blocks, arrived, measured, sample_mask, order, table, partial)


def partner(block, axis, bit):
    count = lax.axis_size(axis)
    route = []
    for low in range(count):
        high = low | 1 << bit
        if high != low and high < count:
            route += [(low, high), (high, low)]
    return lax.ppermute(block, axis, route)


def padded_2(shard, sides, width):
    for axis, dim in sides:
        size, length = (lax.axis_size(axis), shard.shape[dim])
        up = [(i, (i + 1) % size) for i in range(size - 1)]
        down = [(j, i) for i, j in up]
        last = lax.slice_in_dim(shard, length - width, length, axis=dim)
        leading = lax.slice_in_dim(shard, 0, width, axis=dim)
        before = lax.ppermute(last, axis, up)
        after = lax.ppermute(leading, axis, down)
        shard = jnp.concatenate([before, shard, after], axis=dim)
    return shard


def unpack_kernel(kernel):
    shaped = kernel.reshape(2, KS, KS, KS, COILS, 2 * COILS)
    return jnp.transpose(shaped, (0, 4, 5, 1, 2, 3))


def tap_matrix(kernel_part):
    real_part = kernel_part[0]
    imag_part = kernel_part[1]
    upper_rows = jnp.concatenate([real_part, -imag_part], axis=1)
    lower_rows = jnp.concatenate([imag_part, real_part], axis=1)
    blocks = jnp.concatenate([upper_rows, lower_rows], axis=0)
    return jnp.transpose(blocks, (2, 3, 0, 4, 1))


def conjugate(values):
    return jnp.concatenate([values[:1], -values[1:]], axis=0)


def convolve(padded, tap_table):
    extent = tap_table.shape[0]
    channel_count = padded.shape[0] * padded.shape[1]
    channels = padded.reshape((channel_count,) + padded.shape[2:])
    size_x = channels.shape[1] - extent + 1
    size_y = channels.shape[2] - extent + 1
    size_z = channels.shape[3] - extent + 1
    out_rows = tap_table.shape[2]
    running = jnp.zeros((out_rows, size_x * size_y * size_z), jnp.float32)
    for offset_x in range(extent):
        for offset_y in range(extent):
            pieces = [
                channels[
                    :,
                    offset_x : offset_x + size_x,
                    offset_y : offset_y + size_y,
                    offset_z : offset_z + size_z,
                ]
                for offset_z in range(extent)
            ]
            stacked = jnp.stack(pieces).reshape(extent * channel_count, size_x * size_y * size_z)
            weights = tap_table[offset_x, offset_y].reshape(out_rows, extent * channel_count)
            running = running + jnp.dot(weights, stacked, preferred_element_type=jnp.float32)
    return running.reshape(2, out_rows // 2, size_x, size_y, size_z)


def mirror_state(values):
    values = values[:, :, ::-1, ::-1, ::-1]
    for bit_place in range(lax.axis_size(("gx", "gy", "gz")).bit_length() - 1):
        values = partner(values, ("gx", "gy", "gz"), bit_place)
    return values


def halo_body(measured, sample_mask, kernel):
    kernel = unpack_kernel(kernel)
    reach = kernel.shape[-1] // 2
    sampled = (sample_mask == 1)[None, None]
    current = jnp.where(sampled, measured, jnp.zeros_like(measured))
    tap_table = tap_matrix(kernel)
    for iteration in range(ITERS):
        joined = jnp.concatenate([current, conjugate(mirror_state(current))], axis=1)
        padded = padded_2(joined, (("gx", 2), ("gy", 3), ("gz", 4)), reach)
        convolved = convolve(padded, tap_table)
        current = jnp.where(sampled, measured.astype(jnp.float32), convolved).astype(jnp.bfloat16)
    return current


def solution(mesh):
    grid = tuple(mesh.shape[axis] for axis in SPACE)
    spec = P(None, "echo", "gx", "gy", "gz")

    def body(measured, sample_mask, kernel):
        parts, coils, local_x, local_y, local_z = measured.shape
        width = grid[0] * local_x * parts * coils
        points = grid[1] * local_y * local_z
        small = width == 256 and grid == (4, 2, 2) and points == 256 and local_y * local_z == 128
        if small:
            return gathered_body(measured, sample_mask, kernel)
        return halo_body(measured, sample_mask, kernel)

    return jax.shard_map(
        body,
        mesh=mesh,
        in_specs=(spec, P(("echo", "gx"), "gy", "gz"), P()),
        out_specs=spec,
        check_vma=False,
    )
```

```python
import functools

import jax
import jax.numpy as jnp
from jax import lax
from jax.experimental import pallas as pl
from jax.experimental.pallas import tpu as pltpu
from jax.sharding import PartitionSpec as P

COILS = 16
KS = 5
STRIDE = COILS + 1
REACH = KS // 2
ITERS = 2
SPACE = ("gx", "gy", "gz")
UNSAMPLED = 2.0 ** 100
LIMIT = 2.0 ** 99
VMEM_LIMIT = 16 * 2 ** 20


def iota(shape, dim):
    return lax.broadcasted_iota(jnp.int32, shape, dim)


def one_hot(flags):
    return jnp.where(flags, 1.0, 0.0).astype(jnp.bfloat16)


def dot(a, b):
    return jnp.dot(a, b, preferred_element_type=jnp.float32)


def dot_nt(a, b):
    return lax.dot_general(a, b, (((1,), (1,)), ((), ())), preferred_element_type=jnp.float32)


def pack_kernel(measured_hbm, mask_hbm, packed_ref, measured_ref, mask_ref, lined, sems):
    copies = [
        pltpu.make_async_copy(measured_hbm, measured_ref, sems.at[0]),
        pltpu.make_async_copy(mask_hbm, mask_ref, sems.at[1]),
    ]
    for copy in copies:
        copy.start()
    for copy in copies:
        copy.wait()
    parts, coils, size_x, size_y, size_z = measured_ref.shape
    channels = parts * coils
    for x in range(size_x):
        values = measured_ref[:, :, x].astype(jnp.float32)
        sampled = (mask_ref[x] == 1)[None, None]
        coded = jnp.where(sampled, values, UNSAMPLED).reshape(channels, size_y, size_z)
        for row in range(channels):
            lined[x, row * (size_y + 1) : row * (size_y + 1) + size_y, :size_z] = coded[row]
    lane_y = iota((channels, size_y * size_z), 1) // size_z
    for x in range(size_x):
        packed = None
        for y in range(size_y):
            piece = lined[x, pl.ds(y, channels, stride=size_y + 1), :]
            if y > 0:
                piece = jnp.where(lane_y == y, pltpu.roll(piece, y * size_z, 1), packed)
            packed = piece
        packed_ref[x * channels : (x + 1) * channels] = packed.astype(jnp.bfloat16)


def flat_kernel(taps_ref, flat):
    coils = COILS
    pair = 2 * coils
    per_tile = 128 // pair
    lane = iota((128, 256), 1)
    source = (lane // 128) * coils + lane % coils
    for c in range(coils):
        pick = one_hot(iota((128, 256), 0) == (c % per_tile) * pair + source)
        tile = (c // per_tile) * 128
        spread = dot(taps_ref[:, tile : tile + 128], pick)
        for half in range(2):
            rows_of_coil = pl.ds(c, taps_ref.shape[0], stride=STRIDE)
            flat[half, rows_of_coil, :] = spread[:, half * 128 : half * 128 + 128]


def write_orders(order):
    rows = order.shape[1]
    row, col = iota((rows, rows), 0), iota((rows, rows), 1)
    order[:rows] = one_hot(row == col)
    order[rows:] = one_hot(rows - 1 - row == col)


def table_kernel(order_x, flat, table):
    size_x = len(order_x)
    coils = COILS
    channels = 2 * coils
    width = size_x * channels
    group = 128 // channels
    imaginary = iota((coils, 128), 1) // coils % 2 == 1
    lane_group = iota((channels, 128), 1) // channels

    def add_taps(step, carry):
        dy, dz = step // KS, step % KS
        for half in range(2):
            mats = []
            for dx in range(KS):
                tap = (dx * KS + dy) * KS + dz
                real = flat[half, pl.ds(2 * tap * STRIDE, coils), :]
                imag = flat[half, pl.ds((2 * tap + 1) * STRIDE, coils), :]
                if half == 0:
                    top = jnp.where(imaginary, -imag, real)
                    low = jnp.where(imaginary, real, imag)
                else:
                    top = jnp.where(imaginary, imag, real)
                    low = jnp.where(imaginary, -real, imag)
                mats.append(jnp.concatenate([top, low], axis=0).astype(jnp.bfloat16))
            known = {}
            zero = jnp.zeros((channels, 128), jnp.bfloat16)
            for row, x_out in enumerate(order_x):
                for j in range(width // 128):
                    at = order_x[j * group : (j + 1) * group]
                    if half == 1:
                        at = [size_x - 1 - a for a in at]
                    which = tuple(a - x_out + REACH if 0 <= a - x_out + REACH < KS else -1 for a in at)
                    if which not in known:
                        block = zero
                        for g, dx in enumerate(which):
                            if dx >= 0:
                                block = jnp.where(lane_group == g, mats[dx], block)
                        known[which] = block
                    lanes = slice(half * width + j * 128, half * width + j * 128 + 128)
                    table[dy, dz, row * channels : (row + 1) * channels, lanes] = known[which]
        return carry

    lax.fori_loop(0, table.shape[0] * KS, add_taps, 0)


def turn_kernel(count_x, count_y, blocks_ref, order, turned):
    at_x, at_y = lax.axis_index(SPACE[0]) // 2, lax.axis_index(SPACE[1])
    field = jnp.concatenate(
        [
            jnp.concatenate([blocks_ref[(at_y ^ gy) * count_x + (at_x ^ gx)] for gy in range(count_y)], axis=1)
            for gx in range(count_x)
        ],
        axis=0,
    )
    turned[...] = dot_nt(order[...], field).astype(jnp.bfloat16)


def load_half(half, local_z, points, mirrored):
    rows, width = half.shape[0] // 2, half.shape[1]
    edge = REACH * local_z
    for number, ref in enumerate((points, mirrored)):
        values = half[number * rows : (number + 1) * rows]
        ref[:edge] = jnp.zeros((edge, width), jnp.bfloat16)
        ref[edge + rows :] = jnp.zeros((edge, width), jnp.bfloat16)
        ref[edge : edge + rows] = jnp.where(values < LIMIT, values, jnp.zeros_like(values))


def pair_taps(ref, rows, local_z, weights):
    total = None
    for dy in range(0, KS, 2):
        both = range(dy, min(dy + 2, KS))
        values = jnp.concatenate([ref[d * local_z : d * local_z + rows] for d in both], axis=1)
        term = dot_nt(values, jnp.concatenate([weights(d) for d in both], axis=1))
        total = term if total is None else total + term
    return total


def own_lanes(width, own_parity):
    parity = lax.axis_index(SPACE[0]) % 2
    return pl.multiple_of((parity if own_parity else 1 - parity) * width, width)


def give(half, local_z, own_z, own_parity, table, points, mirrored):
    rows, width = half.shape[0] // 2, half.shape[1]
    load_half(half, local_z, points, mirrored)
    first = own_lanes(width, own_parity)

    def given(target, dz):
        number = target if own_z else 1 - target
        lanes = pl.ds(pl.multiple_of(number * table.shape[3] // 2 + first, width), width)
        ref = mirrored if number else points
        return pair_taps(ref, rows, local_z, lambda dy: table[dy, dz, :, lanes])

    return given


def near_kernel(local_z, half, table, partial, points, mirrored):
    given = give(half, local_z, True, True, table, points, mirrored)
    for target in range(2):
        for dz in range(KS):
            partial[target, dz] = given(target, dz)


def more_kernel(local_z, own_z, own_parity, half, table, before, partial, points, mirrored):
    given = give(half, local_z, own_z, own_parity, table, points, mirrored)
    for target in range(2):
        for dz in range(KS):
            partial[target, dz] = before[target, dz] + given(target, dz)


def shift_z(own, other, shift, local_z, dim, own_first):
    length = own.shape[dim]
    inside = iota(own.shape, dim) % local_z + shift
    inside = (inside >= 0) & (inside < local_z)
    across = pltpu.roll(other, (local_z - shift if shift > 0 else -local_z - shift) % length, dim)
    keep = own_first if shift > 0 else 1.0 - own_first
    return jnp.where(inside, pltpu.roll(own, -shift % length, dim), across * keep)


def grid_kernel(
    near_own, near_other, far_own, far_other, measured_ref, mask_ref, order, table, partial,
    out_ref, points, mirrored, coded_ref, near, far, near_mirrored, far_mirrored, lined,
):
    parts, coils, local_x, local_y, local_z = out_ref.shape
    channels = parts * coils
    rows, width = near_own.shape[0] // 2, 2 * near_own.shape[1]
    at_x, at_y = lax.axis_index(SPACE[0]), lax.axis_index(SPACE[1])
    at_x = at_x % 2 * (lax.axis_size(SPACE[0]) // 2) + at_x // 2
    own_first = (1 - lax.axis_index(SPACE[2])).astype(jnp.float32)
    edge = REACH * local_z
    given = give(far_other, local_z, False, False, table, points, mirrored)
    for number, halves in enumerate(((near_own, near_other), (far_own, far_other))):
        for half, own_parity in zip(halves, (True, False)):
            coded_ref[number, :, pl.ds(own_lanes(width // 2, own_parity), width // 2)] = half[:rows]
    for ref in (near, far, near_mirrored, far_mirrored):
        ref[:edge] = jnp.zeros((edge, width), jnp.bfloat16)
        ref[edge + rows :] = jnp.zeros((edge, width), jnp.bfloat16)
    for iteration in range(ITERS - 1):
        totals = [None, None]
        for dz in sorted(range(KS), key=lambda dz: dz == REACH):
            shift = dz - REACH
            own, other = (partial[target, dz] + given(target, dz) for target in range(2))
            if shift != 0:
                own, other = (
                    shift_z(own, other, shift, local_z, 0, own_first),
                    shift_z(other, own, shift, local_z, 0, 1.0 - own_first),
                )
            totals = [part if total is None else total + part for total, part in zip(totals, (own, other))]
        halves = ((near, far_mirrored, coded_ref.at[0], totals[0]), (far, near_mirrored, coded_ref.at[1], totals[1]))
        for ref, mirror_ref, coded, total in halves:
            coded = coded[...]
            values = jnp.where(coded < LIMIT, coded, total.astype(jnp.bfloat16))
            ref[edge : edge + rows] = values
            mirror_ref[edge : edge + rows] = dot(order[rows:], values).astype(jnp.bfloat16)

    own_rows = local_x * channels
    own_points = local_y * local_z
    start_x = pl.multiple_of(at_x * own_rows, own_rows)
    result = None
    for first, refs in ((0, (near, far)), (width, (near_mirrored, far_mirrored))):
        for dy in range(KS):
            taps = [table[dy, dz, pl.ds(start_x, own_rows), first : first + width] for dz in range(KS)]
            start = pl.multiple_of((at_y * local_y + dy) * local_z, local_z)
            window = jnp.concatenate([ref[pl.ds(start, own_points), :] for ref in refs], axis=0)
            term = dot_nt(jnp.concatenate(taps, axis=0), window)
            result = term if result is None else result + term
    total = None
    for dz in range(KS):
        own = result[dz * own_rows : (dz + 1) * own_rows, :own_points]
        other = result[dz * own_rows : (dz + 1) * own_rows, own_points:]
        if dz != REACH:
            own = shift_z(own, other, dz - REACH, local_z, 1, own_first)
        total = own if total is None else total + own

    for y in range(local_y):
        piece = total if y == 0 else pltpu.roll(total, own_points - y * local_z, 1)
        lined[pl.ds(y, own_rows, stride=local_y + 1), :] = piece
    for x in range(local_x):
        starts = [row * (local_y + 1) for row in range(x * channels, (x + 1) * channels)]
        values = jnp.stack([lined[start : start + local_y, :local_z] for start in starts])
        values = values.reshape(parts, coils, local_y, local_z)
        sampled = (mask_ref[x] == 1)[None, None]
        values = jnp.where(sampled, measured_ref[:, :, x].astype(jnp.float32), values)
        out_ref[:, :, x] = values.astype(jnp.bfloat16)


def swap(block, axis, bit):
    count = lax.axis_size(axis)
    return lax.ppermute(block, axis, [(i, i ^ bit) for i in range(count)])


def gathered_body(measured, sample_mask, kernel):
    parts, coils, local_x, local_y, local_z = measured.shape
    sizes = tuple(lax.axis_size(axis) for axis in SPACE)
    devices = sizes[0] * sizes[1] * sizes[2]
    channels = parts * coils
    size_x, size_y, size_z = sizes[0] * local_x, sizes[1] * local_y, sizes[2] * local_z
    width = size_x * channels
    half_rows = size_y * local_z
    in_vmem = pl.BlockSpec(memory_space=pltpu.VMEM)
    in_hbm = pl.BlockSpec(memory_space=pltpu.HBM)

    def call(kernel_fn, name, out_shape, in_specs, scratch=(), outs=1, cost=2 ** 22):
        return pl.pallas_call(
            kernel_fn,
            out_shape=out_shape,
            in_specs=in_specs,
            out_specs=in_vmem if outs == 1 else (in_vmem,) * outs,
            scratch_shapes=list(scratch),
            compiler_params=pltpu.CompilerParams(vmem_limit_bytes=VMEM_LIMIT),
            cost_estimate=pl.CostEstimate(flops=0, bytes_accessed=cost, transcendentals=0),
            name=name,
        )

    packed = call(
        pack_kernel,
        "pack",
        jax.ShapeDtypeStruct((local_x * channels, local_y * local_z), jnp.bfloat16),
        [in_hbm, in_hbm],
        [
            pltpu.VMEM(measured.shape, measured.dtype),
            pltpu.VMEM(sample_mask.shape, sample_mask.dtype),
            pltpu.VMEM((local_x, channels * (local_y + 1), local_y * local_z), jnp.float32),
            pltpu.SemaphoreType.DMA((2,)),
        ],
    )(*[pltpu.with_memory_space_constraint(a, pltpu.HBM) for a in (measured, sample_mask)])

    def after(arrived, *work):
        return lax.optimization_barrier((arrived,) + work)

    taps = jnp.moveaxis(kernel, 0, 3).reshape(parts * KS ** 3, coils * 2 * coils)
    taps = jnp.pad(taps, ((0, -taps.shape[0] % 16), (0, 0)))
    bits = [[(axis, 1 << bit) for bit in range(lax.axis_size(axis).bit_length() - 1)] for axis in SPACE]
    steps = bits[0][1:] + bits[1] + bits[0][:1] + bits[2]
    order_x = [gx * local_x + x for odd in range(2) for gx in range(odd, sizes[0], 2) for x in range(local_x)]
    half_x = sizes[0] // 2
    padded_rows = half_rows + 2 * REACH * local_z
    padded_part = pltpu.VMEM((padded_rows, width // 2), jnp.bfloat16)
    padded = pltpu.VMEM((padded_rows, width), jnp.bfloat16)
    partial_shape = jax.ShapeDtypeStruct((2, KS, half_rows, width), jnp.float32)
    scratch = [padded_part, padded_part]

    def more(own_z, own_parity, half, table, before):
        more_fn = functools.partial(more_kernel, local_z, own_z, own_parity)
        return call(more_fn, "more", partial_shape, [in_vmem] * 3, scratch)(half, table, before)

    blocks = packed[None]
    for number, (axis, bit) in enumerate(steps):
        arrived = swap(blocks, axis, bit)
        if number == 0:
            flat_shape = jax.ShapeDtypeStruct((2, taps.shape[0] * STRIDE, 128), jnp.float32)
            arrived, flat = after(arrived, call(flat_kernel, "flat", flat_shape, [in_vmem])(taps))
        elif number == 1:
            order_shape = jax.ShapeDtypeStruct((2 * half_rows, half_rows), jnp.bfloat16)
            order = call(write_orders, "order", order_shape, [])()
            table_shape = jax.ShapeDtypeStruct((KS, KS, width, 2 * width), jnp.bfloat16)
            table = call(functools.partial(table_kernel, order_x), "table", table_shape, [in_vmem])(flat)
            arrived, table, order = after(arrived, table, order)
        elif number == 2:
            turned_shape = jax.ShapeDtypeStruct((2 * half_rows, width // 2), jnp.bfloat16)
            turn_fn = functools.partial(turn_kernel, half_x, sizes[1])
            turned = call(turn_fn, "turn", turned_shape, [in_vmem] * 2)(blocks, order)
            turned_far = swap(turned, SPACE[2], 1)
            near_fn = functools.partial(near_kernel, local_z)
            partial = call(near_fn, "near", partial_shape, [in_vmem] * 2, scratch)(turned, table)
            turned_far, partial = after(turned_far, partial)
            partial = more(False, True, turned_far, table, partial)
            arrived, turned, turned_far, partial = after(arrived, turned, turned_far, partial)
            blocks = call(turn_fn, "turn_other", turned_shape, [in_vmem] * 2)(arrived, order)
            continue
        elif number == 3:
            partial = more(True, False, blocks, table, partial)
            arrived, partial = after(arrived, partial)
            break
        blocks = jnp.concatenate([blocks, arrived], axis=0)

    lined = pltpu.VMEM((local_x * channels * (local_y + 1), 128), jnp.float32)
    return call(
        grid_kernel,
        "grid",
        jax.ShapeDtypeStruct(measured.shape, jnp.bfloat16),
        [in_vmem] * 9,
        scratch + [pltpu.VMEM((2, half_rows, width), jnp.bfloat16)] + [padded] * 4 + [lined],
    )(turned, blocks, turned_far, arrived, measured, sample_mask, order, table, partial)


def partner(block, axis, bit):
    count = lax.axis_size(axis)
    route = []
    for low in range(count):
        high = low | 1 << bit
        if high != low and high < count:
            route += [(low, high), (high, low)]
    return lax.ppermute(block, axis, route)


def padded_2(shard, sides, width):
    for axis, dim in sides:
        size, length = (lax.axis_size(axis), shard.shape[dim])
        up = [(i, (i + 1) % size) for i in range(size - 1)]
        down = [(j, i) for i, j in up]
        last = lax.slice_in_dim(shard, length - width, length, axis=dim)
        leading = lax.slice_in_dim(shard, 0, width, axis=dim)
        before = lax.ppermute(last, axis, up)
        after = lax.ppermute(leading, axis, down)
        shard = jnp.concatenate([before, shard, after], axis=dim)
    return shard


def unpack_kernel(kernel):
    shaped = kernel.reshape(2, KS, KS, KS, COILS, 2 * COILS)
    return jnp.transpose(shaped, (0, 4, 5, 1, 2, 3))


def tap_matrix(kernel_part):
    real_part = kernel_part[0]
    imag_part = kernel_part[1]
    upper_rows = jnp.concatenate([real_part, -imag_part], axis=1)
    lower_rows = jnp.concatenate([imag_part, real_part], axis=1)
    blocks = jnp.concatenate([upper_rows, lower_rows], axis=0)
    return jnp.transpose(blocks, (2, 3, 0, 4, 1))


def conjugate(values):
    return jnp.concatenate([values[:1], -values[1:]], axis=0)


def convolve(padded, tap_table):
    extent = tap_table.shape[0]
    channel_count = padded.shape[0] * padded.shape[1]
    channels = padded.reshape((channel_count,) + padded.shape[2:])
    size_x = channels.shape[1] - extent + 1
    size_y = channels.shape[2] - extent + 1
    size_z = channels.shape[3] - extent + 1
    out_rows = tap_table.shape[2]
    running = jnp.zeros((out_rows, size_x * size_y * size_z), jnp.float32)
    for offset_x in range(extent):
        for offset_y in range(extent):
            pieces = [
                channels[
                    :,
                    offset_x : offset_x + size_x,
                    offset_y : offset_y + size_y,
                    offset_z : offset_z + size_z,
                ]
                for offset_z in range(extent)
            ]
            stacked = jnp.stack(pieces).reshape(extent * channel_count, size_x * size_y * size_z)
            weights = tap_table[offset_x, offset_y].reshape(out_rows, extent * channel_count)
            running = running + jnp.dot(weights, stacked, preferred_element_type=jnp.float32)
    return running.reshape(2, out_rows // 2, size_x, size_y, size_z)


def mirror_state(values):
    values = values[:, :, ::-1, ::-1, ::-1]
    for bit_place in range(lax.axis_size(("gx", "gy", "gz")).bit_length() - 1):
        values = partner(values, ("gx", "gy", "gz"), bit_place)
    return values


def halo_body(measured, sample_mask, kernel):
    kernel = unpack_kernel(kernel)
    reach = kernel.shape[-1] // 2
    sampled = (sample_mask == 1)[None, None]
    current = jnp.where(sampled, measured, jnp.zeros_like(measured))
    tap_table = tap_matrix(kernel)
    for iteration in range(ITERS):
        joined = jnp.concatenate([current, conjugate(mirror_state(current))], axis=1)
        padded = padded_2(joined, (("gx", 2), ("gy", 3), ("gz", 4)), reach)
        convolved = convolve(padded, tap_table)
        current = jnp.where(sampled, measured.astype(jnp.float32), convolved).astype(jnp.bfloat16)
    return current


def solution(mesh):
    grid = tuple(mesh.shape[axis] for axis in SPACE)
    spec = P(None, "echo", "gx", "gy", "gz")

    def body(measured, sample_mask, kernel):
        parts, coils, local_x, local_y, local_z = measured.shape
        width = grid[0] * local_x * parts * coils
        points = grid[1] * local_y * local_z
        small = width == 256 and grid == (4, 2, 2) and points == 256 and local_y * local_z == 128
        if small:
            return gathered_body(measured, sample_mask, kernel)
        return halo_body(measured, sample_mask, kernel)

    return jax.shard_map(
        body,
        mesh=mesh,
        in_specs=(spec, P(("echo", "gx"), "gy", "gz"), P()),
        out_specs=spec,
        check_vma=False,
    )
```

```python
import functools

import jax
import jax.numpy as jnp
from jax import lax
from jax.experimental import pallas as pl
from jax.experimental.pallas import tpu as pltpu
from jax.sharding import PartitionSpec as P


COILS = 16
KS = 5
STRIDE = COILS + 1
REACH = KS // 2
ITERS = 2
SPACE = ("gx", "gy", "gz")
UNSAMPLED = 2.0 ** 100
LIMIT = 2.0 ** 99
VMEM_LIMIT = 16 * 2 ** 20


def iota(shape, dim):
    return lax.broadcasted_iota(jnp.int32, shape, dim)


def one_hot(flags):
    return jnp.where(flags, 1.0, 0.0).astype(jnp.bfloat16)


def dot(a, b):
    return jnp.dot(a, b, preferred_element_type=jnp.float32)


def dot_nt(a, b):
    return lax.dot_general(a, b, (((1,), (1,)), ((), ())), preferred_element_type=jnp.float32)


def pack_kernel(measured_hbm, mask_hbm, packed_ref, measured_ref, mask_ref, lined, sems):
    copies = [
        pltpu.make_async_copy(measured_hbm, measured_ref, sems.at[0]),
        pltpu.make_async_copy(mask_hbm, mask_ref, sems.at[1]),
    ]
    for copy in copies:
        copy.start()
    for copy in copies:
        copy.wait()
    parts, coils, size_x, size_y, size_z = measured_ref.shape
    channels = parts * coils
    for x in range(size_x):
        values = measured_ref[:, :, x].astype(jnp.float32)
        sampled = (mask_ref[x] == 1)[None, None]
        coded = jnp.where(sampled, values, UNSAMPLED).reshape(channels, size_y, size_z)
        for row in range(channels):
            lined[x, row * (size_y + 1) : row * (size_y + 1) + size_y, :size_z] = coded[row]
    lane_y = iota((channels, size_y * size_z), 1) // size_z
    for x in range(size_x):
        packed = None
        for y in range(size_y):
            piece = lined[x, pl.ds(y, channels, stride=size_y + 1), :]
            if y > 0:
                piece = jnp.where(lane_y == y, pltpu.roll(piece, y * size_z, 1), packed)
            packed = piece
        packed_ref[x * channels : (x + 1) * channels] = packed.astype(jnp.bfloat16)


def flat_kernel(taps_ref, flat):
    coils = COILS
    pair = 2 * coils
    per_tile = 128 // pair
    lane = iota((128, 256), 1)
    source = (lane // 128) * coils + lane % coils
    for c in range(coils):
        pick = one_hot(iota((128, 256), 0) == (c % per_tile) * pair + source)
        tile = (c // per_tile) * 128
        spread = dot(taps_ref[:, tile : tile + 128], pick)
        for half in range(2):
            rows_of_coil = pl.ds(c, taps_ref.shape[0], stride=STRIDE)
            flat[half, rows_of_coil, :] = spread[:, half * 128 : half * 128 + 128]


def write_orders(order):
    rows = order.shape[1]
    row, col = iota((rows, rows), 0), iota((rows, rows), 1)
    order[:rows] = one_hot(row == col)
    order[rows:] = one_hot(rows - 1 - row == col)


def table_kernel(order_x, flat, table):
    size_x = len(order_x)
    coils = COILS
    channels = 2 * coils
    width = size_x * channels
    group = 128 // channels
    imaginary = iota((coils, 128), 1) // coils % 2 == 1
    lane_group = iota((channels, 128), 1) // channels

    def add_taps(step, carry):
        dy, dz = step // KS, step % KS
        for half in range(2):
            mats = []
            for dx in range(KS):
                tap = (dx * KS + dy) * KS + dz
                real = flat[half, pl.ds(2 * tap * STRIDE, coils), :]
                imag = flat[half, pl.ds((2 * tap + 1) * STRIDE, coils), :]
                if half == 0:
                    top = jnp.where(imaginary, -imag, real)
                    low = jnp.where(imaginary, real, imag)
                else:
                    top = jnp.where(imaginary, imag, real)
                    low = jnp.where(imaginary, -real, imag)
                mats.append(jnp.concatenate([top, low], axis=0).astype(jnp.bfloat16))
            known = {}
            zero = jnp.zeros((channels, 128), jnp.bfloat16)
            for row, x_out in enumerate(order_x):
                for j in range(width // 128):
                    at = order_x[j * group : (j + 1) * group]
                    if half == 1:
                        at = [size_x - 1 - a for a in at]
                    which = tuple(a - x_out + REACH if 0 <= a - x_out + REACH < KS else -1 for a in at)
                    if which not in known:
                        block = zero
                        for g, dx in enumerate(which):
                            if dx >= 0:
                                block = jnp.where(lane_group == g, mats[dx], block)
                        known[which] = block
                    lanes = slice(half * width + j * 128, half * width + j * 128 + 128)
                    table[dy, dz, row * channels : (row + 1) * channels, lanes] = known[which]
        return carry

    lax.fori_loop(0, table.shape[0] * KS, add_taps, 0)


def turn_kernel(count_x, count_y, blocks_ref, order, turned):
    at_x, at_y = lax.axis_index(SPACE[0]) // 2, lax.axis_index(SPACE[1])
    field = jnp.concatenate(
        [
            jnp.concatenate([blocks_ref[(at_y ^ gy) * count_x + (at_x ^ gx)] for gy in range(count_y)], axis=1)
            for gx in range(count_x)
        ],
        axis=0,
    )
    turned[...] = dot_nt(order[...], field).astype(jnp.bfloat16)


def load_half(half, local_z, points, mirrored):
    rows, width = half.shape[0] // 2, half.shape[1]
    edge = REACH * local_z
    for number, ref in enumerate((points, mirrored)):
        values = half[number * rows : (number + 1) * rows]
        ref[:edge] = jnp.zeros((edge, width), jnp.bfloat16)
        ref[edge + rows :] = jnp.zeros((edge, width), jnp.bfloat16)
        ref[edge : edge + rows] = jnp.where(values < LIMIT, values, jnp.zeros_like(values))


def pair_taps(ref, rows, local_z, weights, count):
    total = None
    for dy in range(0, count, 2):
        both = range(dy, min(dy + 2, count))
        values = jnp.concatenate([ref[d * local_z : d * local_z + rows] for d in both], axis=1)
        term = dot_nt(values, jnp.concatenate([weights(d) for d in both], axis=1))
        total = term if total is None else total + term
    return total


def own_lanes(width, own_parity):
    parity = lax.axis_index(SPACE[0]) % 2
    return pl.multiple_of((parity if own_parity else 1 - parity) * width, width)


def give(half, local_z, own_z, own_parity, table, points, mirrored, count=KS):
    rows, width = half.shape[0] // 2, half.shape[1]
    load_half(half, local_z, points, mirrored)
    first = own_lanes(width, own_parity)

    def given(target, dz):
        number = target if own_z else 1 - target
        lanes = pl.ds(pl.multiple_of(number * table.shape[3] // 2 + first, width), width)
        ref = mirrored if number else points
        return pair_taps(ref, rows, local_z, lambda dy: table[dy, dz, :, lanes], count)

    return given


def near_kernel(local_z, half, table, partial, points, mirrored):
    given = give(half, local_z, True, True, table, points, mirrored)
    for target in range(2):
        for dz in range(KS):
            partial[target, dz] = given(target, dz)


def more_kernel(local_z, own_z, own_parity, half, table, before, partial, points, mirrored):
    given = give(half, local_z, own_z, own_parity, table, points, mirrored, KS if own_z else KS - 1)
    for target in range(2):
        for dz in range(KS):
            partial[target, dz] = before[target, dz] + given(target, dz)


def shift_z(own, other, shift, local_z, dim, own_first):
    length = own.shape[dim]
    inside = iota(own.shape, dim) % local_z + shift
    inside = (inside >= 0) & (inside < local_z)
    across = pltpu.roll(other, (local_z - shift if shift > 0 else -local_z - shift) % length, dim)
    keep = own_first if shift > 0 else 1.0 - own_first
    return jnp.where(inside, pltpu.roll(own, -shift % length, dim), across * keep)


def grid_kernel(
    near_own, near_other, far_own, far_other, measured_ref, mask_ref, order, table, partial,
    out_ref, points, mirrored, points_own, mirrored_own, coded_ref, near, far, near_mirrored, far_mirrored, lined,
):
    parts, coils, local_x, local_y, local_z = out_ref.shape
    channels = parts * coils
    rows, width = near_own.shape[0] // 2, 2 * near_own.shape[1]
    at_x, at_y = lax.axis_index(SPACE[0]), lax.axis_index(SPACE[1])
    at_x = at_x % 2 * (lax.axis_size(SPACE[0]) // 2) + at_x // 2
    own_first = (1 - lax.axis_index(SPACE[2])).astype(jnp.float32)
    edge = REACH * local_z
    given = give(far_other, local_z, False, False, table, points, mirrored, KS - 1)
    load_half(far_own, local_z, points_own, mirrored_own)
    last = slice((KS - 1) * local_z, (KS - 1) * local_z + rows)
    pairs = ((mirrored_own, mirrored), (points_own, points))
    last_values = [jnp.concatenate([ref[last] for ref in pair], axis=1) for pair in pairs]

    def last_given(target, dz):
        part = width // 2
        lanes = [(1 - target) * width + own_lanes(part, own_parity) for own_parity in (True, False)]
        weights = [table[KS - 1, dz, :, pl.ds(pl.multiple_of(at, part), part)] for at in lanes]
        return dot_nt(last_values[target], jnp.concatenate(weights, axis=1))

    for number, halves in enumerate(((near_own, near_other), (far_own, far_other))):
        for half, own_parity in zip(halves, (True, False)):
            coded_ref[number, :, pl.ds(own_lanes(width // 2, own_parity), width // 2)] = half[:rows]
    for ref in (near, far, near_mirrored, far_mirrored):
        ref[:edge] = jnp.zeros((edge, width), jnp.bfloat16)
        ref[edge + rows :] = jnp.zeros((edge, width), jnp.bfloat16)
    for _ in range(ITERS - 1):
        totals = [None, None]
        for dz in sorted(range(KS), key=lambda dz: dz == REACH):
            shift = dz - REACH
            own, other = (
                partial[target, dz] + given(target, dz) + last_given(target, dz) for target in range(2)
            )
            if shift != 0:
                own, other = (
                    shift_z(own, other, shift, local_z, 0, own_first),
                    shift_z(other, own, shift, local_z, 0, 1.0 - own_first),
                )
            totals = [part if total is None else total + part for total, part in zip(totals, (own, other))]
        halves = ((near, far_mirrored, coded_ref.at[0], totals[0]), (far, near_mirrored, coded_ref.at[1], totals[1]))
        for ref, mirror_ref, coded, total in halves:
            coded = coded[...]
            values = jnp.where(coded < LIMIT, coded, total.astype(jnp.bfloat16))
            ref[edge : edge + rows] = values
            mirror_ref[edge : edge + rows] = dot(order[rows:], values).astype(jnp.bfloat16)

    own_rows = local_x * channels
    own_points = local_y * local_z
    start_x = pl.multiple_of(at_x * own_rows, own_rows)
    result = None
    for first, refs in ((0, (near, far)), (width, (near_mirrored, far_mirrored))):
        for dy in range(KS):
            taps = [table[dy, dz, pl.ds(start_x, own_rows), first : first + width] for dz in range(KS)]
            start = pl.multiple_of((at_y * local_y + dy) * local_z, local_z)
            window = jnp.concatenate([ref[pl.ds(start, own_points), :] for ref in refs], axis=0)
            term = dot_nt(jnp.concatenate(taps, axis=0), window)
            result = term if result is None else result + term
    total = None
    for dz in range(KS):
        own = result[dz * own_rows : (dz + 1) * own_rows, :own_points]
        other = result[dz * own_rows : (dz + 1) * own_rows, own_points:]
        if dz != REACH:
            own = shift_z(own, other, dz - REACH, local_z, 1, own_first)
        total = own if total is None else total + own

    for y in range(local_y):
        piece = total if y == 0 else pltpu.roll(total, own_points - y * local_z, 1)
        lined[pl.ds(y, own_rows, stride=local_y + 1), :] = piece
    for x in range(local_x):
        starts = [row * (local_y + 1) for row in range(x * channels, (x + 1) * channels)]
        values = jnp.stack([lined[start : start + local_y, :local_z] for start in starts])
        values = values.reshape(parts, coils, local_y, local_z)
        sampled = (mask_ref[x] == 1)[None, None]
        values = jnp.where(sampled, measured_ref[:, :, x].astype(jnp.float32), values)
        out_ref[:, :, x] = values.astype(jnp.bfloat16)


def swap(block, axis, bit):
    count = lax.axis_size(axis)
    return lax.ppermute(block, axis, [(i, i ^ bit) for i in range(count)])


def gathered_body(measured, sample_mask, kernel):
    parts, coils, local_x, local_y, local_z = measured.shape
    sizes = tuple(lax.axis_size(axis) for axis in SPACE)
    channels = parts * coils
    size_x, size_y = sizes[0] * local_x, sizes[1] * local_y
    width = size_x * channels
    half_rows = size_y * local_z
    in_vmem = pl.BlockSpec(memory_space=pltpu.VMEM)
    in_hbm = pl.BlockSpec(memory_space=pltpu.HBM)

    def call(kernel_fn, out_shape, in_specs, scratch=(), outs=1, cost=2 ** 22):
        return pl.pallas_call(
            kernel_fn,
            out_shape=out_shape,
            in_specs=in_specs,
            out_specs=in_vmem if outs == 1 else (in_vmem,) * outs,
            scratch_shapes=list(scratch),
            compiler_params=pltpu.CompilerParams(vmem_limit_bytes=VMEM_LIMIT),
            cost_estimate=pl.CostEstimate(flops=0, bytes_accessed=cost, transcendentals=0),
        )

    packed = call(
        pack_kernel,
        jax.ShapeDtypeStruct((local_x * channels, local_y * local_z), jnp.bfloat16),
        [in_hbm, in_hbm],
        [
            pltpu.VMEM(measured.shape, measured.dtype),
            pltpu.VMEM(sample_mask.shape, sample_mask.dtype),
            pltpu.VMEM((local_x, channels * (local_y + 1), local_y * local_z), jnp.float32),
            pltpu.SemaphoreType.DMA((2,)),
        ],
    )(*[pltpu.with_memory_space_constraint(a, pltpu.HBM) for a in (measured, sample_mask)])

    def after(arrived, *work):
        return lax.optimization_barrier((arrived,) + work)

    taps = jnp.moveaxis(kernel, 0, 3).reshape(parts * KS ** 3, coils * 2 * coils)
    taps = jnp.pad(taps, ((0, -taps.shape[0] % 16), (0, 0)))
    bits = [[(axis, 1 << bit) for bit in range(lax.axis_size(axis).bit_length() - 1)] for axis in SPACE]
    steps = bits[0][1:] + bits[1] + bits[0][:1] + bits[2]
    order_x = [gx * local_x + x for odd in range(2) for gx in range(odd, sizes[0], 2) for x in range(local_x)]
    half_x = sizes[0] // 2
    padded_rows = half_rows + 2 * REACH * local_z
    padded_part = pltpu.VMEM((padded_rows, width // 2), jnp.bfloat16)
    padded = pltpu.VMEM((padded_rows, width), jnp.bfloat16)
    partial_shape = jax.ShapeDtypeStruct((2, KS, half_rows, width), jnp.float32)
    scratch = [padded_part, padded_part]

    def more(own_z, own_parity, half, table, before):
        more_fn = functools.partial(more_kernel, local_z, own_z, own_parity)
        return call(more_fn, partial_shape, [in_vmem] * 3, scratch)(half, table, before)

    blocks = packed[None]
    for number, (axis, bit) in enumerate(steps):
        arrived = swap(blocks, axis, bit)
        if number == 0:
            flat_shape = jax.ShapeDtypeStruct((2, taps.shape[0] * STRIDE, 128), jnp.float32)
            arrived, flat = after(arrived, call(flat_kernel, flat_shape, [in_vmem])(taps))
        elif number == 1:
            order_shape = jax.ShapeDtypeStruct((2 * half_rows, half_rows), jnp.bfloat16)
            order = call(write_orders, order_shape, [])()
            table_shape = jax.ShapeDtypeStruct((KS, KS, width, 2 * width), jnp.bfloat16)
            table = call(functools.partial(table_kernel, order_x), table_shape, [in_vmem])(flat)
            arrived, table, order = after(arrived, table, order)
        elif number == 2:
            turned_shape = jax.ShapeDtypeStruct((2 * half_rows, width // 2), jnp.bfloat16)
            turn_fn = functools.partial(turn_kernel, half_x, sizes[1])
            turned = call(turn_fn, turned_shape, [in_vmem] * 2)(blocks, order)
            turned_far = swap(turned, SPACE[2], 1)
            near_fn = functools.partial(near_kernel, local_z)
            partial = call(near_fn, partial_shape, [in_vmem] * 2, scratch)(turned, table)
            turned_far, partial = after(turned_far, partial)
            partial = more(False, True, turned_far, table, partial)
            arrived, turned, turned_far, partial = after(arrived, turned, turned_far, partial)
            blocks = call(turn_fn, turned_shape, [in_vmem] * 2)(arrived, order)
            continue
        elif number == 3:
            partial = more(True, False, blocks, table, partial)
            arrived, partial = after(arrived, partial)
            break
        blocks = jnp.concatenate([blocks, arrived], axis=0)

    lined = pltpu.VMEM((local_x * channels * (local_y + 1), 128), jnp.float32)
    return call(
        grid_kernel,
        jax.ShapeDtypeStruct(measured.shape, jnp.bfloat16),
        [in_vmem] * 9,
        scratch * 2 + [pltpu.VMEM((2, half_rows, width), jnp.bfloat16)] + [padded] * 4 + [lined],
    )(turned, blocks, turned_far, arrived, measured, sample_mask, order, table, partial)


def partner(block, axis, bit):
    count = lax.axis_size(axis)
    route = []
    for low in range(count):
        high = low | 1 << bit
        if high != low and high < count:
            route += [(low, high), (high, low)]
    return lax.ppermute(block, axis, route)


def padded_2(shard, sides, width):
    for axis, dim in sides:
        size, length = (lax.axis_size(axis), shard.shape[dim])
        up = [(i, (i + 1) % size) for i in range(size - 1)]
        down = [(j, i) for i, j in up]
        last = lax.slice_in_dim(shard, length - width, length, axis=dim)
        leading = lax.slice_in_dim(shard, 0, width, axis=dim)
        before = lax.ppermute(last, axis, up)
        after = lax.ppermute(leading, axis, down)
        shard = jnp.concatenate([before, shard, after], axis=dim)
    return shard


def unpack_kernel(kernel):
    shaped = kernel.reshape(2, KS, KS, KS, COILS, 2 * COILS)
    return jnp.transpose(shaped, (0, 4, 5, 1, 2, 3))


def tap_matrix(kernel_part):
    real_part = kernel_part[0]
    imag_part = kernel_part[1]
    upper_rows = jnp.concatenate([real_part, -imag_part], axis=1)
    lower_rows = jnp.concatenate([imag_part, real_part], axis=1)
    blocks = jnp.concatenate([upper_rows, lower_rows], axis=0)
    return jnp.transpose(blocks, (2, 3, 0, 4, 1))


def conjugate(values):
    return jnp.concatenate([values[:1], -values[1:]], axis=0)


def convolve(padded, tap_table):
    extent = tap_table.shape[0]
    channel_count = padded.shape[0] * padded.shape[1]
    channels = padded.reshape((channel_count,) + padded.shape[2:])
    size_x = channels.shape[1] - extent + 1
    size_y = channels.shape[2] - extent + 1
    size_z = channels.shape[3] - extent + 1
    out_rows = tap_table.shape[2]
    running = jnp.zeros((out_rows, size_x * size_y * size_z), jnp.float32)
    for offset_x in range(extent):
        for offset_y in range(extent):
            pieces = [
                channels[
                    :,
                    offset_x : offset_x + size_x,
                    offset_y : offset_y + size_y,
                    offset_z : offset_z + size_z,
                ]
                for offset_z in range(extent)
            ]
            stacked = jnp.stack(pieces).reshape(extent * channel_count, size_x * size_y * size_z)
            weights = tap_table[offset_x, offset_y].reshape(out_rows, extent * channel_count)
            running = running + jnp.dot(weights, stacked, preferred_element_type=jnp.float32)
    return running.reshape(2, out_rows // 2, size_x, size_y, size_z)


def mirror_state(values):
    values = values[:, :, ::-1, ::-1, ::-1]
    for bit_place in range(lax.axis_size(("gx", "gy", "gz")).bit_length() - 1):
        values = partner(values, ("gx", "gy", "gz"), bit_place)
    return values


def halo_body(measured, sample_mask, kernel):
    kernel = unpack_kernel(kernel)
    reach = kernel.shape[-1] // 2
    sampled = (sample_mask == 1)[None, None]
    current = jnp.where(sampled, measured, jnp.zeros_like(measured))
    tap_table = tap_matrix(kernel)
    for _ in range(ITERS):
        joined = jnp.concatenate([current, conjugate(mirror_state(current))], axis=1)
        padded = padded_2(joined, (("gx", 2), ("gy", 3), ("gz", 4)), reach)
        convolved = convolve(padded, tap_table)
        current = jnp.where(sampled, measured.astype(jnp.float32), convolved).astype(jnp.bfloat16)
    return current


def solution(mesh):
    grid = tuple(mesh.shape[axis] for axis in SPACE)
    spec = P(None, "echo", "gx", "gy", "gz")

    def body(measured, sample_mask, kernel):
        parts, coils, local_x, local_y, local_z = measured.shape
        width = grid[0] * local_x * parts * coils
        points = grid[1] * local_y * local_z
        small = width == 256 and grid == (4, 2, 2) and points == 256 and local_y * local_z == 128
        if small:
            return gathered_body(measured, sample_mask, kernel)
        return halo_body(measured, sample_mask, kernel)

    return jax.shard_map(
        body,
        mesh=mesh,
        in_specs=(spec, P(("echo", "gx"), "gy", "gz"), P()),
        out_specs=spec,
        check_vma=False,
    )
```

```python
import functools

import jax
import jax.numpy as jnp
from jax import lax
from jax.experimental import pallas as pl
from jax.experimental.pallas import tpu as pltpu
from jax.sharding import PartitionSpec as P


COILS = 16
KS = 5
STRIDE = COILS + 1
REACH = KS // 2
ITERS = 2
SPACE = ("gx", "gy", "gz")
UNSAMPLED = 2.0 ** 100
LIMIT = 2.0 ** 99
VMEM_LIMIT = 16 * 2 ** 20


def iota(shape, dim):
    return lax.broadcasted_iota(jnp.int32, shape, dim)


def one_hot(flags):
    return jnp.where(flags, 1.0, 0.0).astype(jnp.bfloat16)


def dot(a, b):
    return jnp.dot(a, b, preferred_element_type=jnp.float32)


def dot_nt(a, b):
    return lax.dot_general(a, b, (((1,), (1,)), ((), ())), preferred_element_type=jnp.float32)


def pack_kernel(measured_hbm, mask_hbm, packed_ref, measured_ref, mask_ref, lined, sems):
    copies = [
        pltpu.make_async_copy(measured_hbm, measured_ref, sems.at[0]),
        pltpu.make_async_copy(mask_hbm, mask_ref, sems.at[1]),
    ]
    for copy in copies:
        copy.start()
    for copy in copies:
        copy.wait()
    parts, coils, size_x, size_y, size_z = measured_ref.shape
    channels = parts * coils
    for x in range(size_x):
        values = measured_ref[:, :, x].astype(jnp.float32)
        sampled = (mask_ref[x] == 1)[None, None]
        coded = jnp.where(sampled, values, UNSAMPLED).reshape(channels, size_y, size_z)
        for row in range(channels):
            lined[x, row * (size_y + 1) : row * (size_y + 1) + size_y, :size_z] = coded[row]
    lane_y = iota((channels, size_y * size_z), 1) // size_z
    for x in range(size_x):
        packed = None
        for y in range(size_y):
            piece = lined[x, pl.ds(y, channels, stride=size_y + 1), :]
            if y > 0:
                piece = jnp.where(lane_y == y, pltpu.roll(piece, y * size_z, 1), packed)
            packed = piece
        packed_ref[x * channels : (x + 1) * channels] = packed.astype(jnp.bfloat16)


def flat_kernel(taps_ref, flat):
    coils = COILS
    pair = 2 * coils
    per_tile = 128 // pair
    lane = iota((128, 256), 1)
    source = (lane // 128) * coils + lane % coils
    for c in range(coils):
        pick = one_hot(iota((128, 256), 0) == (c % per_tile) * pair + source)
        tile = (c // per_tile) * 128
        spread = dot(taps_ref[:, tile : tile + 128], pick)
        for half in range(2):
            rows_of_coil = pl.ds(c, taps_ref.shape[0], stride=STRIDE)
            flat[half, rows_of_coil, :] = spread[:, half * 128 : half * 128 + 128]


def write_orders(order):
    rows = order.shape[1]
    row, col = iota((rows, rows), 0), iota((rows, rows), 1)
    order[:rows] = one_hot(row == col)
    order[rows:] = one_hot(rows - 1 - row == col)


def table_kernel(order_x, flat, table):
    size_x = len(order_x)
    coils = COILS
    channels = 2 * coils
    width = size_x * channels
    group = 128 // channels
    imaginary = iota((coils, 128), 1) // coils % 2 == 1
    lane_group = iota((channels, 128), 1) // channels

    def add_taps(step, carry):
        dy, dz = step // KS, step % KS
        for half in range(2):
            mats = []
            for dx in range(KS):
                tap = (dx * KS + dy) * KS + dz
                real = flat[half, pl.ds(2 * tap * STRIDE, coils), :]
                imag = flat[half, pl.ds((2 * tap + 1) * STRIDE, coils), :]
                if half == 0:
                    top = jnp.where(imaginary, -imag, real)
                    low = jnp.where(imaginary, real, imag)
                else:
                    top = jnp.where(imaginary, imag, real)
                    low = jnp.where(imaginary, -real, imag)
                mats.append(jnp.concatenate([top, low], axis=0).astype(jnp.bfloat16))
            known = {}
            zero = jnp.zeros((channels, 128), jnp.bfloat16)
            for row, x_out in enumerate(order_x):
                for j in range(width // 128):
                    at = order_x[j * group : (j + 1) * group]
                    if half == 1:
                        at = [size_x - 1 - a for a in at]
                    which = tuple(a - x_out + REACH if 0 <= a - x_out + REACH < KS else -1 for a in at)
                    if which not in known:
                        block = zero
                        for g, dx in enumerate(which):
                            if dx >= 0:
                                block = jnp.where(lane_group == g, mats[dx], block)
                        known[which] = block
                    lanes = slice(half * width + j * 128, half * width + j * 128 + 128)
                    table[dy, dz, row * channels : (row + 1) * channels, lanes] = known[which]
        return carry

    lax.fori_loop(0, table.shape[0] * KS, add_taps, 0)


def turn_kernel(count_x, count_y, blocks_ref, order, turned):
    at_x, at_y = lax.axis_index(SPACE[0]) // 2, lax.axis_index(SPACE[1])
    field = jnp.concatenate(
        [
            jnp.concatenate([blocks_ref[(at_y ^ gy) * count_x + (at_x ^ gx)] for gy in range(count_y)], axis=1)
            for gx in range(count_x)
        ],
        axis=0,
    )
    turned[...] = dot_nt(order[...], field).astype(jnp.bfloat16)


def load_half(half, local_z, points, mirrored):
    rows, width = half.shape[0] // 2, half.shape[1]
    edge = REACH * local_z
    for number, ref in enumerate((points, mirrored)):
        values = half[number * rows : (number + 1) * rows]
        ref[:edge] = jnp.zeros((edge, width), jnp.bfloat16)
        ref[edge + rows :] = jnp.zeros((edge, width), jnp.bfloat16)
        ref[edge : edge + rows] = jnp.where(values < LIMIT, values, jnp.zeros_like(values))


def pair_taps(ref, rows, local_z, weights, count):
    total = None
    for dy in range(0, count, 2):
        both = range(dy, min(dy + 2, count))
        values = jnp.concatenate([ref[d * local_z : d * local_z + rows] for d in both], axis=1)
        term = dot_nt(values, jnp.concatenate([weights(d) for d in both], axis=1))
        total = term if total is None else total + term
    return total


def own_lanes(width, own_parity):
    parity = lax.axis_index(SPACE[0]) % 2
    return pl.multiple_of((parity if own_parity else 1 - parity) * width, width)


def give(half, local_z, own_z, own_parity, table, points, mirrored, count=KS):
    rows, width = half.shape[0] // 2, half.shape[1]
    load_half(half, local_z, points, mirrored)
    first = own_lanes(width, own_parity)

    def given(target, dz):
        number = target if own_z else 1 - target
        lanes = pl.ds(pl.multiple_of(number * table.shape[3] // 2 + first, width), width)
        ref = mirrored if number else points
        return pair_taps(ref, rows, local_z, lambda dy: table[dy, dz, :, lanes], count)

    return given


def near_kernel(local_z, half, table, partial, points, mirrored):
    given = give(half, local_z, True, True, table, points, mirrored)
    for target in range(2):
        for dz in range(KS):
            partial[target, dz] = given(target, dz)


def more_kernel(local_z, own_z, own_parity, half, table, before, partial, points, mirrored):
    given = give(half, local_z, own_z, own_parity, table, points, mirrored, KS if own_z else KS - 1)
    for target in range(2):
        for dz in range(KS):
            partial[target, dz] = before[target, dz] + given(target, dz)


def shift_z(own, other, shift, local_z, dim, own_first):
    length = own.shape[dim]
    inside = iota(own.shape, dim) % local_z + shift
    inside = (inside >= 0) & (inside < local_z)
    across = pltpu.roll(other, (local_z - shift if shift > 0 else -local_z - shift) % length, dim)
    keep = own_first if shift > 0 else 1.0 - own_first
    return jnp.where(inside, pltpu.roll(own, -shift % length, dim), across * keep)


def grid_kernel(
    near_own, near_other, far_own, far_other, measured_ref, mask_ref, order, table, partial,
    out_ref, points, mirrored, points_own, mirrored_own, coded_ref, near, far, near_mirrored, far_mirrored, lined,
):
    parts, coils, local_x, local_y, local_z = out_ref.shape
    channels = parts * coils
    rows, width = near_own.shape[0] // 2, 2 * near_own.shape[1]
    at_x, at_y = lax.axis_index(SPACE[0]), lax.axis_index(SPACE[1])
    at_x = at_x % 2 * (lax.axis_size(SPACE[0]) // 2) + at_x // 2
    own_first = (1 - lax.axis_index(SPACE[2])).astype(jnp.float32)
    edge = REACH * local_z
    given = give(far_other, local_z, False, False, table, points, mirrored, KS - 1)
    load_half(far_own, local_z, points_own, mirrored_own)
    last = slice((KS - 1) * local_z, (KS - 1) * local_z + rows)
    pairs = ((mirrored_own, mirrored), (points_own, points))
    last_values = [jnp.concatenate([ref[last] for ref in pair], axis=1) for pair in pairs]

    def last_given(target, dz):
        part = width // 2
        lanes = [(1 - target) * width + own_lanes(part, own_parity) for own_parity in (True, False)]
        weights = [table[KS - 1, dz, :, pl.ds(pl.multiple_of(at, part), part)] for at in lanes]
        return dot_nt(last_values[target], jnp.concatenate(weights, axis=1))

    for number, halves in enumerate(((near_own, near_other), (far_own, far_other))):
        for half, own_parity in zip(halves, (True, False)):
            coded_ref[number, :, pl.ds(own_lanes(width // 2, own_parity), width // 2)] = half[:rows]
    for ref in (near, far, near_mirrored, far_mirrored):
        ref[:edge] = jnp.zeros((edge, width), jnp.bfloat16)
        ref[edge + rows :] = jnp.zeros((edge, width), jnp.bfloat16)
    for iteration in range(ITERS - 1):
        totals = [None, None]
        for dz in sorted(range(KS), key=lambda dz: dz == REACH):
            shift = dz - REACH
            own, other = (
                partial[target, dz] + given(target, dz) + last_given(target, dz) for target in range(2)
            )
            if shift != 0:
                own, other = (
                    shift_z(own, other, shift, local_z, 0, own_first),
                    shift_z(other, own, shift, local_z, 0, 1.0 - own_first),
                )
            totals = [part if total is None else total + part for total, part in zip(totals, (own, other))]
        halves = ((near, far_mirrored, coded_ref.at[0], totals[0]), (far, near_mirrored, coded_ref.at[1], totals[1]))
        for ref, mirror_ref, coded, total in halves:
            coded = coded[...]
            values = jnp.where(coded < LIMIT, coded, total.astype(jnp.bfloat16))
            ref[edge : edge + rows] = values
            mirror_ref[edge : edge + rows] = dot(order[rows:], values).astype(jnp.bfloat16)

    own_rows = local_x * channels
    own_points = local_y * local_z
    start_x = pl.multiple_of(at_x * own_rows, own_rows)
    result = None
    for first, refs in ((0, (near, far)), (width, (near_mirrored, far_mirrored))):
        for dy in range(KS):
            taps = [table[dy, dz, pl.ds(start_x, own_rows), first : first + width] for dz in range(KS)]
            start = pl.multiple_of((at_y * local_y + dy) * local_z, local_z)
            window = jnp.concatenate([ref[pl.ds(start, own_points), :] for ref in refs], axis=0)
            term = dot_nt(jnp.concatenate(taps, axis=0), window)
            result = term if result is None else result + term
    total = None
    for dz in range(KS):
        own = result[dz * own_rows : (dz + 1) * own_rows, :own_points]
        other = result[dz * own_rows : (dz + 1) * own_rows, own_points:]
        if dz != REACH:
            own = shift_z(own, other, dz - REACH, local_z, 1, own_first)
        total = own if total is None else total + own

    for y in range(local_y):
        piece = total if y == 0 else pltpu.roll(total, own_points - y * local_z, 1)
        lined[pl.ds(y, own_rows, stride=local_y + 1), :] = piece
    for x in range(local_x):
        starts = [row * (local_y + 1) for row in range(x * channels, (x + 1) * channels)]
        values = jnp.stack([lined[start : start + local_y, :local_z] for start in starts])
        values = values.reshape(parts, coils, local_y, local_z)
        sampled = (mask_ref[x] == 1)[None, None]
        values = jnp.where(sampled, measured_ref[:, :, x].astype(jnp.float32), values)
        out_ref[:, :, x] = values.astype(jnp.bfloat16)


def swap(block, axis, bit):
    count = lax.axis_size(axis)
    return lax.ppermute(block, axis, [(i, i ^ bit) for i in range(count)])


def gathered_body(measured, sample_mask, kernel):
    parts, coils, local_x, local_y, local_z = measured.shape
    sizes = tuple(lax.axis_size(axis) for axis in SPACE)
    devices = sizes[0] * sizes[1] * sizes[2]
    channels = parts * coils
    size_x, size_y, size_z = sizes[0] * local_x, sizes[1] * local_y, sizes[2] * local_z
    width = size_x * channels
    half_rows = size_y * local_z
    in_vmem = pl.BlockSpec(memory_space=pltpu.VMEM)
    in_hbm = pl.BlockSpec(memory_space=pltpu.HBM)

    def call(kernel_fn, name, out_shape, in_specs, scratch=(), outs=1, cost=2 ** 22):
        return pl.pallas_call(
            kernel_fn,
            out_shape=out_shape,
            in_specs=in_specs,
            out_specs=in_vmem if outs == 1 else (in_vmem,) * outs,
            scratch_shapes=list(scratch),
            compiler_params=pltpu.CompilerParams(vmem_limit_bytes=VMEM_LIMIT),
            cost_estimate=pl.CostEstimate(flops=0, bytes_accessed=cost, transcendentals=0),
            name=name,
        )

    packed = call(
        pack_kernel,
        "pack",
        jax.ShapeDtypeStruct((local_x * channels, local_y * local_z), jnp.bfloat16),
        [in_hbm, in_hbm],
        [
            pltpu.VMEM(measured.shape, measured.dtype),
            pltpu.VMEM(sample_mask.shape, sample_mask.dtype),
            pltpu.VMEM((local_x, channels * (local_y + 1), local_y * local_z), jnp.float32),
            pltpu.SemaphoreType.DMA((2,)),
        ],
    )(*[pltpu.with_memory_space_constraint(a, pltpu.HBM) for a in (measured, sample_mask)])

    def after(arrived, *work):
        return lax.optimization_barrier((arrived,) + work)

    taps = jnp.moveaxis(kernel, 0, 3).reshape(parts * KS ** 3, coils * 2 * coils)
    taps = jnp.pad(taps, ((0, -taps.shape[0] % 16), (0, 0)))
    bits = [[(axis, 1 << bit) for bit in range(lax.axis_size(axis).bit_length() - 1)] for axis in SPACE]
    steps = bits[0][1:] + bits[1] + bits[0][:1] + bits[2]
    order_x = [gx * local_x + x for odd in range(2) for gx in range(odd, sizes[0], 2) for x in range(local_x)]
    half_x = sizes[0] // 2
    padded_rows = half_rows + 2 * REACH * local_z
    padded_part = pltpu.VMEM((padded_rows, width // 2), jnp.bfloat16)
    padded = pltpu.VMEM((padded_rows, width), jnp.bfloat16)
    partial_shape = jax.ShapeDtypeStruct((2, KS, half_rows, width), jnp.float32)
    scratch = [padded_part, padded_part]

    def more(own_z, own_parity, half, table, before):
        more_fn = functools.partial(more_kernel, local_z, own_z, own_parity)
        return call(more_fn, "more", partial_shape, [in_vmem] * 3, scratch)(half, table, before)

    blocks = packed[None]
    for number, (axis, bit) in enumerate(steps):
        with jax.named_scope(f"step_{number}"):
            arrived = swap(blocks, axis, bit)
        if number == 0:
            arrived, taps = after(arrived, taps)
        elif number == 1:
            flat_shape = jax.ShapeDtypeStruct((2, taps.shape[0] * STRIDE, 128), jnp.float32)
            flat = call(flat_kernel, "flat", flat_shape, [in_vmem])(taps)
            order_shape = jax.ShapeDtypeStruct((2 * half_rows, half_rows), jnp.bfloat16)
            order = call(write_orders, "order", order_shape, [])()
            table_shape = jax.ShapeDtypeStruct((KS, KS, width, 2 * width), jnp.bfloat16)
            table = call(functools.partial(table_kernel, order_x), "table", table_shape, [in_vmem])(flat)
            arrived, table, order = after(arrived, table, order)
        elif number == 2:
            turned_shape = jax.ShapeDtypeStruct((2 * half_rows, width // 2), jnp.bfloat16)
            turn_fn = functools.partial(turn_kernel, half_x, sizes[1])
            with jax.named_scope("turn_own"):
                turned = call(turn_fn, "turn", turned_shape, [in_vmem] * 2)(blocks, order)
            turned_far = swap(turned, SPACE[2], 1)
            near_fn = functools.partial(near_kernel, local_z)
            partial = call(near_fn, "near", partial_shape, [in_vmem] * 2, scratch)(turned, table)
            turned_far, partial = after(turned_far, partial)
            partial = more(False, True, turned_far, table, partial)
            arrived, turned, turned_far, partial = after(arrived, turned, turned_far, partial)
            blocks = call(turn_fn, "turn_other", turned_shape, [in_vmem] * 2)(arrived, order)
            continue
        elif number == 3:
            partial = more(True, False, blocks, table, partial)
            arrived, partial = after(arrived, partial)
            break
        blocks = jnp.concatenate([blocks, arrived], axis=0)

    lined = pltpu.VMEM((local_x * channels * (local_y + 1), 128), jnp.float32)
    return call(
        grid_kernel,
        "grid",
        jax.ShapeDtypeStruct(measured.shape, jnp.bfloat16),
        [in_vmem] * 9,
        scratch * 2 + [pltpu.VMEM((2, half_rows, width), jnp.bfloat16)] + [padded] * 4 + [lined],
    )(turned, blocks, turned_far, arrived, measured, sample_mask, order, table, partial)


def partner(block, axis, bit):
    count = lax.axis_size(axis)
    route = []
    for low in range(count):
        high = low | 1 << bit
        if high != low and high < count:
            route += [(low, high), (high, low)]
    return lax.ppermute(block, axis, route)


def padded_2(shard, sides, width):
    for axis, dim in sides:
        size, length = (lax.axis_size(axis), shard.shape[dim])
        up = [(i, (i + 1) % size) for i in range(size - 1)]
        down = [(j, i) for i, j in up]
        last = lax.slice_in_dim(shard, length - width, length, axis=dim)
        leading = lax.slice_in_dim(shard, 0, width, axis=dim)
        before = lax.ppermute(last, axis, up)
        after = lax.ppermute(leading, axis, down)
        shard = jnp.concatenate([before, shard, after], axis=dim)
    return shard


def unpack_kernel(kernel):
    shaped = kernel.reshape(2, KS, KS, KS, COILS, 2 * COILS)
    return jnp.transpose(shaped, (0, 4, 5, 1, 2, 3))


def tap_matrix(kernel_part):
    real_part = kernel_part[0]
    imag_part = kernel_part[1]
    upper_rows = jnp.concatenate([real_part, -imag_part], axis=1)
    lower_rows = jnp.concatenate([imag_part, real_part], axis=1)
    blocks = jnp.concatenate([upper_rows, lower_rows], axis=0)
    return jnp.transpose(blocks, (2, 3, 0, 4, 1))


def conjugate(values):
    return jnp.concatenate([values[:1], -values[1:]], axis=0)


def convolve(padded, tap_table):
    extent = tap_table.shape[0]
    channel_count = padded.shape[0] * padded.shape[1]
    channels = padded.reshape((channel_count,) + padded.shape[2:])
    size_x = channels.shape[1] - extent + 1
    size_y = channels.shape[2] - extent + 1
    size_z = channels.shape[3] - extent + 1
    out_rows = tap_table.shape[2]
    running = jnp.zeros((out_rows, size_x * size_y * size_z), jnp.float32)
    for offset_x in range(extent):
        for offset_y in range(extent):
            pieces = [
                channels[
                    :,
                    offset_x : offset_x + size_x,
                    offset_y : offset_y + size_y,
                    offset_z : offset_z + size_z,
                ]
                for offset_z in range(extent)
            ]
            stacked = jnp.stack(pieces).reshape(extent * channel_count, size_x * size_y * size_z)
            weights = tap_table[offset_x, offset_y].reshape(out_rows, extent * channel_count)
            running = running + jnp.dot(weights, stacked, preferred_element_type=jnp.float32)
    return running.reshape(2, out_rows // 2, size_x, size_y, size_z)


def mirror_state(values):
    values = values[:, :, ::-1, ::-1, ::-1]
    for bit_place in range(lax.axis_size(("gx", "gy", "gz")).bit_length() - 1):
        values = partner(values, ("gx", "gy", "gz"), bit_place)
    return values


def halo_body(measured, sample_mask, kernel):
    kernel = unpack_kernel(kernel)
    reach = kernel.shape[-1] // 2
    sampled = (sample_mask == 1)[None, None]
    current = jnp.where(sampled, measured, jnp.zeros_like(measured))
    tap_table = tap_matrix(kernel)
    for iteration in range(ITERS):
        joined = jnp.concatenate([current, conjugate(mirror_state(current))], axis=1)
        padded = padded_2(joined, (("gx", 2), ("gy", 3), ("gz", 4)), reach)
        convolved = convolve(padded, tap_table)
        current = jnp.where(sampled, measured.astype(jnp.float32), convolved).astype(jnp.bfloat16)
    return current


def solution(mesh):
    grid = tuple(mesh.shape[axis] for axis in SPACE)
    spec = P(None, "echo", "gx", "gy", "gz")

    def body(measured, sample_mask, kernel):
        parts, coils, local_x, local_y, local_z = measured.shape
        width = grid[0] * local_x * parts * coils
        points = grid[1] * local_y * local_z
        small = width == 256 and grid == (4, 2, 2) and points == 256 and local_y * local_z == 128
        if small:
            return gathered_body(measured, sample_mask, kernel)
        return halo_body(measured, sample_mask, kernel)

    return jax.shard_map(
        body,
        mesh=mesh,
        in_specs=(spec, P(("echo", "gx"), "gy", "gz"), P()),
        out_specs=spec,
        check_vma=False,
    )
```
